128 devices in a mesh: sec: 4 (over y_hi, core), dev: 32 (over z, y_lo, x).
Axes of the slice: x: 4, y: 4 (y_hi: 2, y_lo: 2; y = y_hi * 2 + y_lo), z: 4, core: 2. Of those that a mesh axis runs over, the one named last changes fastest.
Arguments:
- queries: bfloat16 [256, 8192], P('dev', 'sec')
- fresh_key_value: bfloat16 [2, 256, 512], P(None, 'dev', 'sec'), may hold values from -6 to 6
- key_value_cache: bfloat16 [2, 256, 1024, 512], P(None, 'dev', None, 'sec'), may hold values from -6 to 6
- lengths: int32 [256], P('dev'), may hold values from 1 to 1024, as said below
- residual: bfloat16 [256, 4096], P(None, 'dev'), may hold values from -6 to 6
- out_weight: bfloat16 [8192, 4096], P('sec', 'dev'), may hold values from -0.0625 to 0.0625
- norm_gain: float32 [4096], P('dev'), may hold values from 0.1 to 1.9
- routes: int32 [256, 8], replicated, may hold values from 0 to 63, all different within a row; in each aligned block of 256 rows (0 to 255, 256 to 511, ...) at most 64 rows name the same one
- route_weights: float32 [256, 8], replicated, may hold values from 0.05 to 0.5
- w_gate: bfloat16 [64, 4096, 1536], P('dev', None, 'sec'), may hold values from -0.09375 to 0.09375
- w_up: bfloat16 [64, 4096, 1536], P('dev', None, 'sec'), may hold values from -0.09375 to 0.09375
- w_down: bfloat16 [64, 1536, 4096], P('dev', 'sec'), may hold values from -0.15625 to 0.15625
Outputs:
- layer_out: bfloat16 [256, 4096], P(None, 'dev')
The draws below stay inside these ranges and needn't reach their ends.
Inputs may be any that keep to these rules, and one draw needn't show every extreme that they name: `routes`: each row names 8 different experts; no expert is named by more than 64 rows, a bound that some block reaches. `lengths`: some row has all 1024 slots filled.
All inputs are finite; a program needn't handle non-finite values.
Results may differ from the reference program's by a relative error of at most 0.0055.
Values may be sent and summed in bfloat16 or wider, within the bound.
No kernel may reach another device: no remote copies, remote signals or barrier semaphores. Data moves between devices by JAX's collectives and lax.ppermute only.
A program may use at most 128 MiB of HBM per device.

```python
import math
import jax
import jax.numpy as jnp
import numpy as np
from jax import lax

D = 4096
QUERY_HEADS = 64
KEY_VALUE_HEADS = 4
HEAD_SIZE = 128
FF = 1536
TOPK = 8
CACHE_SLOTS = 1024
BATCH_ROWS = 256
EXPERTS = 64
CAP = 64


def draw_queries(key, part):
    normal_key = jax.random.fold_in(key, 0)
    values = jax.random.normal(normal_key, (BATCH_ROWS, QUERY_HEADS * HEAD_SIZE), jnp.float32)
    return values.astype(jnp.bfloat16)


def draw_lengths(key, part):
    base_key, spot_key = jax.random.split(key)
    drawn = jax.random.randint(base_key, (BATCH_ROWS,), 1, CACHE_SLOTS + 1, dtype=jnp.int32)
    chosen_row = jax.random.randint(spot_key, (), 0, BATCH_ROWS, dtype=jnp.int32)
    return jnp.where(jnp.arange(BATCH_ROWS, dtype=jnp.int32) == chosen_row, CACHE_SLOTS, drawn).astype(jnp.int32)


def block_levels(key, shape, cuts, low, top_value):
    level = 1.0
    for position, shards_of in cuts:
        heights = jax.random.uniform(jax.random.fold_in(jax.random.fold_in(key, 6), position), (shards_of,), jnp.float32, low / len(cuts), top_value / len(cuts))
        level = level * jnp.repeat(jnp.exp(heights), shape[position] // shards_of).reshape((-1,) + (1,) * (len(shape) - 1 - position))
    return level


def deal_out(key, own, number, rows, amount, top, most, skew):
    order = jax.random.permutation(key, amount)
    heavy_load, ordinary = portions_of(amount, rows * top, most, skew, True), portions_of(amount, rows * top, most, skew, False)
    places = jnp.arange(amount)

    def named(tallies, offset_by):
        used = int((tallies > 0).sum())
        fixed = max(1, used // 4)
        shifted = fixed + (places - fixed + offset_by * (used - fixed)) % max(1, amount - fixed)
        return jnp.zeros((amount,), jnp.int32).at[order[jnp.where(places < fixed, places, shifted)]].set(jnp.asarray(tallies, jnp.int32))

    tallies = jnp.where(number % 4 == 0, named(heavy_load, number // 4), named(ordinary, number - number // 4 - 1))
    mixed = jax.random.permutation(jax.random.fold_in(own, 3), amount)
    source_of, taker = mixed[0:amount // 2 * 2:2], mixed[1:amount // 2 * 2:2]
    margin = jnp.minimum(tallies[source_of] - 1, most - tallies[taker]) // 2
    margin = jnp.where((source_of == order[0]) | (taker == order[0]) | (tallies[taker] == 0), 0, jnp.maximum(margin, 0))
    shifted = jax.random.randint(jax.random.fold_in(own, 4), (amount // 2,), 0, 1 << 20) % (margin + 1)
    tallies = tallies.at[source_of].add(-shifted).at[taker].add(shifted)
    labels = jnp.searchsorted(jnp.cumsum(tallies), jnp.arange(rows * top), side="right").astype(jnp.int32)
    table = labels.reshape(top, rows).T
    table = table[jax.random.permutation(jax.random.fold_in(own, 1), rows)]
    offset_by = jax.random.randint(jax.random.fold_in(own, 2), (rows, 1), 0, top)
    return jnp.take_along_axis(table, (jnp.arange(top)[None, :] + offset_by) % top, axis=1)


def portions_of(count, total, most, skew, full):
    portions = [(1 << 20) // math.isqrt(rank ** skew) + 1 for rank in range(1, count + 1)]
    largest = most if full else min(most, max(-(-total // count), total * portions[0] // sum(portions)))
    least = 1 if total - largest >= count - 1 else 0
    given, spare = [largest] + [least] * (count - 1), total - largest - least * (count - 1)
    while spare > 0:
        movable = [i for i in range(1, count) if given[i] < largest] or [i for i in range(1, count) if given[i] < most]
        pool, budget = sum([portions[i] for i in movable]), spare
        for i in movable:
            more = min(most - given[i], max(1, budget * portions[i] // pool), spare)
            given[i] = given[i] + more
            spare = spare - more
    return np.array(given)


def bell_draw(rng, extent, scale, reach, shards=(), held_as=jnp.bfloat16):
    gain = block_levels(rng, extent, shards, -0.22, 0.18) if shards else 1.0
    values = jax.random.normal(rng, extent, jnp.float32) * scale * gain
    return jnp.minimum(jnp.maximum(values, -reach), reach).astype(held_as)


def setup_inputs(seed: int = 0) -> dict:
    keys = jax.random.split(jax.random.key(seed), 13)
    queries = draw_queries(jax.random.fold_in(keys[12], 71), 0)
    fresh_key_value = bell_draw(keys[1], (2, BATCH_ROWS, KEY_VALUE_HEADS * HEAD_SIZE), 1.0, 6.0, ((1, 32), (2, 4)))
    key_value_cache = bell_draw(keys[2], (2, BATCH_ROWS, CACHE_SLOTS, KEY_VALUE_HEADS * HEAD_SIZE), 1.0, 6.0, ((1, 32), (3, 4)))
    lengths = draw_lengths(jax.random.fold_in(keys[12], 71), 0)
    residual = bell_draw(keys[4], (BATCH_ROWS, D), 1.0, 6.0, ((1, 32),))
    out_weight = bell_draw(keys[5], (QUERY_HEADS * HEAD_SIZE, D), (QUERY_HEADS * HEAD_SIZE) ** -0.5, 0.0625, ((0, 4), (1, 32)))
    norm_gain = jnp.clip(1.0 + 0.18 * jax.random.normal(keys[6], (D,), jnp.float32), 0.1, 1.9)
    routes_keys = jax.random.split(jax.random.fold_in(keys[7], 1), BATCH_ROWS // BATCH_ROWS)
    routes_turns = jax.random.permutation(jax.random.fold_in(keys[7], 3), BATCH_ROWS // BATCH_ROWS)
    routes = jax.vmap(lambda own, number: deal_out(jax.random.fold_in(keys[7], 2), own, number, BATCH_ROWS, EXPERTS, TOPK, CAP, 2))(routes_keys, routes_turns).reshape((BATCH_ROWS, TOPK))
    route_weights = jnp.clip(jnp.exp(jax.random.uniform(keys[8], (BATCH_ROWS, TOPK), jnp.float32, math.log(0.05), math.log(0.5))), 0.05, 0.5)
    w_gate = bell_draw(keys[9], (EXPERTS, D, FF), D ** -0.5, 0.09375, ((0, 32), (2, 4)))
    w_up = bell_draw(keys[10], (EXPERTS, D, FF), D ** -0.5, 0.09375, ((0, 32), (2, 4)))
    w_down = bell_draw(keys[11], (EXPERTS, FF, D), FF ** -0.5, 0.15625, ((0, 32), (1, 4)))
    return dict(queries=queries, fresh_key_value=fresh_key_value, key_value_cache=key_value_cache, lengths=lengths, residual=residual, out_weight=out_weight, norm_gain=norm_gain, routes=routes, route_weights=route_weights, w_gate=w_gate, w_up=w_up, w_down=w_down)


def reference(queries, fresh_key_value, key_value_cache, lengths, residual, out_weight, norm_gain, routes, route_weights, w_gate, w_up, w_down):
    queries_per_group = QUERY_HEADS // KEY_VALUE_HEADS
    score_scale = 1.0 / math.sqrt(HEAD_SIZE)
    visible = jnp.arange(CACHE_SLOTS, dtype=jnp.int32)[None, :] < lengths[:, None]
    visible_mask = visible[:, None, :]
    outputs = []
    for key_value_head in range(KEY_VALUE_HEADS):
        head_queries = queries[:, key_value_head * queries_per_group * HEAD_SIZE:(key_value_head + 1) * queries_per_group * HEAD_SIZE]
        head_queries = head_queries.reshape(BATCH_ROWS, queries_per_group, HEAD_SIZE).astype(jnp.float32)
        cached_keys = key_value_cache[0, :, :, key_value_head * HEAD_SIZE:(key_value_head + 1) * HEAD_SIZE].astype(jnp.float32)
        cached_values = key_value_cache[1, :, :, key_value_head * HEAD_SIZE:(key_value_head + 1) * HEAD_SIZE].astype(jnp.float32)
        own_key = fresh_key_value[0, :, key_value_head * HEAD_SIZE:(key_value_head + 1) * HEAD_SIZE].astype(jnp.float32)
        own_value = fresh_key_value[1, :, key_value_head * HEAD_SIZE:(key_value_head + 1) * HEAD_SIZE].astype(jnp.float32)
        scores = jnp.einsum('rgd,rtd->rgt', head_queries, cached_keys) * score_scale
        own_score = jnp.einsum('rgd,rd->rg', head_queries, own_key) * score_scale
        row_max = jnp.maximum(lax.optimization_barrier(jnp.max(jnp.where(visible_mask, scores, -jnp.inf), axis=-1)), own_score)
        weights = jnp.where(visible_mask, jnp.exp(scores - row_max[..., None]), 0.0)
        own_weight = jnp.exp(own_score - row_max)
        normalizer = lax.optimization_barrier(jnp.sum(weights, axis=-1)) + own_weight
        rounded = lax.optimization_barrier(weights.astype(jnp.bfloat16)).astype(jnp.float32)
        weighted = jnp.einsum('rgt,rtd->rgd', rounded, cached_values) + own_weight[..., None] * own_value[:, None, :]
        outputs.append((weighted / normalizer[..., None]).reshape(BATCH_ROWS, queries_per_group * HEAD_SIZE))
    attn = jnp.concatenate(outputs, axis=1).astype(jnp.bfloat16)
    hidden = residual.astype(jnp.float32) + jnp.dot(attn, out_weight, preferred_element_type=jnp.float32)
    mean_square = lax.optimization_barrier(jnp.mean(hidden * hidden, axis=-1, keepdims=True))
    normed = (hidden * lax.rsqrt(mean_square + 1e-06) * norm_gain).astype(jnp.bfloat16)
    slot_ids = jnp.arange(CAP, dtype=jnp.int32)

    def one_expert(carry, inputs):
        expert, gate_w, up_w, down_w = inputs
        matches = routes == expert
        chosen = jnp.any(matches, axis=1)
        shares = lax.optimization_barrier(jnp.sum(jnp.where(matches, route_weights, 0.0), axis=1))
        slot_rank = jnp.cumsum(chosen.astype(jnp.int32)) - 1
        slot_mask = chosen[None, :] & (slot_rank[None, :] == slot_ids[:, None])
        picked = jnp.dot(slot_mask.astype(jnp.bfloat16), normed, preferred_element_type=jnp.float32).astype(jnp.bfloat16)
        gate_part = jnp.dot(picked, gate_w, preferred_element_type=jnp.float32)
        upward = jnp.dot(picked, up_w, preferred_element_type=jnp.float32)
        activation = (jax.nn.silu(gate_part) * upward).astype(jnp.bfloat16)
        result = jnp.dot(activation, down_w, preferred_element_type=jnp.float32)
        spread = slot_mask.astype(jnp.float32) * shares[None, :]
        return (carry + jnp.dot(spread.T, result, precision=lax.Precision.HIGHEST), None)
    mixture, _ = lax.scan(one_expert, jnp.zeros((BATCH_ROWS, D), jnp.float32), (jnp.arange(EXPERTS, dtype=jnp.int32), w_gate, w_up, w_down))
    return (hidden + mixture).astype(jnp.bfloat16)
```

```python
import math

import jax
import jax.numpy as jnp
from jax import lax
from jax.sharding import PartitionSpec as P

D = 4096
QUERY_HEADS = 64
KEY_VALUE_HEADS = 4
HEAD_SIZE = 128
CAP = 64
GROUPS = 32
CORE_SWAP = [(0, 1), (1, 0), (2, 3), (3, 2)]


def attend(queries, fresh_key_value, key_value_cache, lengths):
    row_count = key_value_cache.shape[1]
    cache_length = key_value_cache.shape[2]
    heads_kv = key_value_cache.shape[3] // HEAD_SIZE
    queries_per_group = QUERY_HEADS // KEY_VALUE_HEADS
    score_scale = 1.0 / math.sqrt(HEAD_SIZE)
    head_queries = queries.reshape(row_count, heads_kv, queries_per_group, HEAD_SIZE)
    cached_keys = key_value_cache[0].reshape(row_count, cache_length, heads_kv, HEAD_SIZE)
    cached_values = key_value_cache[1].reshape(row_count, cache_length, heads_kv, HEAD_SIZE)
    own_key = fresh_key_value[0].reshape(row_count, heads_kv, HEAD_SIZE)
    own_value = fresh_key_value[1].reshape(row_count, heads_kv, HEAD_SIZE).astype(jnp.float32)
    scores = (
        jnp.einsum("rkgd,rtkd->rkgt", head_queries, cached_keys, preferred_element_type=jnp.float32)
        * score_scale
    )
    own_score = (
        jnp.einsum("rkgd,rkd->rkg", head_queries, own_key, preferred_element_type=jnp.float32)
        * score_scale
    )
    visible = (jnp.arange(cache_length, dtype=jnp.int32)[None, :] < lengths[:, None])[
        :, None, None, :
    ]
    row_max = jnp.maximum(jnp.max(jnp.where(visible, scores, -jnp.inf), axis=-1), own_score)
    weights = jnp.where(visible, jnp.exp(scores - row_max[..., None]), 0.0)
    own_weight = jnp.exp(own_score - row_max)
    normalizer = jnp.sum(weights, axis=-1) + own_weight
    weighted = jnp.einsum(
        "rkgt,rtkd->rkgd",
        weights.astype(jnp.bfloat16),
        cached_values,
        preferred_element_type=jnp.float32,
    )
    weighted = weighted + own_weight[..., None] * own_value[:, :, None, :]
    return (
        (weighted / normalizer[..., None])
        .astype(jnp.bfloat16)
        .reshape(row_count, heads_kv * queries_per_group * HEAD_SIZE)
    )


def three_terms(values):
    high = lax.reduce_precision(values, 8, 7)
    rest = values - high
    middle = lax.reduce_precision(rest, 8, 7)
    low = rest - middle
    return jnp.stack([high, middle, low]).astype(jnp.bfloat16)


def exchange(blocks):
    return lax.all_to_all(blocks, "dev", 0, 0, tiled=True)


def slot_tables(routes):
    expert_ids = jnp.arange(2 * GROUPS, dtype=jnp.int32)
    chosen = jnp.any(routes[:, :, None] == expert_ids, axis=1)
    earlier = jnp.tri(routes.shape[0], k=-1, dtype=jnp.bfloat16)
    rank = jnp.dot(earlier, chosen.astype(jnp.bfloat16), preferred_element_type=jnp.float32)
    return jnp.where(chosen, rank.astype(jnp.int32), -1).T


def one_hot(ranks):
    slot_ids = jnp.arange(CAP, dtype=jnp.int32)[None, :, None]
    return (ranks[:, None, :] == slot_ids).astype(jnp.bfloat16)


def shards(
    queries,
    fresh_key_value,
    key_value_cache,
    lengths,
    residual,
    out_weight,
    norm_gain,
    routes,
    route_weights,
    w_gate,
    w_up,
    w_down,
):
    row_count = routes.shape[0]
    core = lax.axis_index("sec") % 2
    group = lax.axis_index("dev")
    attn = attend(queries, fresh_key_value, key_value_cache, lengths)
    gain_rows = jnp.pad(three_terms(norm_gain), ((0, attn.shape[0] - 3), (0, 0)))
    block = jnp.concatenate([attn, gain_rows], axis=1)
    gathered = exchange(jnp.broadcast_to(block, (GROUPS,) + block.shape))
    gain = jnp.sum(gathered[:, :3, attn.shape[1] :].astype(jnp.float32), axis=1)
    partial_out = jnp.dot(
        gathered[:, :, : attn.shape[1]].reshape(row_count, attn.shape[1]),
        out_weight,
        preferred_element_type=jnp.float32,
    )
    hidden = residual.astype(jnp.float32) + jnp.sum(lax.all_gather(partial_out, "sec"), axis=0)

    ranks = slot_tables(routes).reshape(GROUPS, 2, row_count)
    own_ranks = lax.dynamic_index_in_dim(ranks, core, 1, keepdims=False)
    other_ranks = lax.dynamic_index_in_dim(ranks, 1 - core, 1, keepdims=False)
    sent = jnp.einsum(
        "ekr,rf->ekf", one_hot(own_ranks), hidden.astype(jnp.bfloat16), preferred_element_type=jnp.float32
    ).astype(jnp.bfloat16)
    own_rows = exchange(sent)
    other_rows = lax.ppermute(own_rows, "sec", CORE_SWAP)

    local_ids = 2 * group + jnp.arange(2, dtype=jnp.int32)
    local_ranks = lax.dynamic_index_in_dim(ranks, group, 0, keepdims=False)
    shares = jnp.sum(
        jnp.where(routes[None] == local_ids[:, None, None], route_weights[None], 0.0), axis=2
    )
    slot_share = jnp.sum(
        jnp.where(
            local_ranks[:, None, :] == jnp.arange(CAP, dtype=jnp.int32)[None, :, None],
            shares[:, None, :],
            0.0,
        ),
        axis=2,
    )

    rows = jnp.where(core == 0, jnp.stack([own_rows, other_rows]), jnp.stack([other_rows, own_rows]))
    rows = rows.astype(jnp.float32)
    square = jnp.sum(rows * rows, axis=(1, 3), keepdims=True)
    normed = rows * lax.rsqrt(square / D + 1e-06) * gain[None, :, None, :]
    picked = normed.astype(jnp.bfloat16).transpose(0, 2, 1, 3).reshape(2, CAP, D)
    gate_part = jnp.einsum("ecd,edf->ecf", picked, w_gate, preferred_element_type=jnp.float32)
    upward = jnp.einsum("ecd,edf->ecf", picked, w_up, preferred_element_type=jnp.float32)
    activation = (jax.nn.silu(gate_part) * upward).astype(jnp.bfloat16)
    result = jnp.einsum("ecf,efd->ecd", activation, w_down, preferred_element_type=jnp.float32)
    result = result * slot_share[:, :, None]
    own_result = lax.dynamic_index_in_dim(result, core, 0, keepdims=False)
    other_result = lax.dynamic_index_in_dim(result, 1 - core, 0, keepdims=False)
    moved = lax.ppermute(own_result.astype(jnp.bfloat16), "sec", CORE_SWAP)
    summed = (other_result + moved.astype(jnp.float32)).astype(jnp.bfloat16)
    returned = exchange(summed.reshape(CAP, GROUPS, D // GROUPS).transpose(1, 0, 2))
    mixture_part = jnp.einsum(
        "ekr,ekf->rf", one_hot(other_ranks), returned, preferred_element_type=jnp.float32
    )
    mixture = jnp.sum(lax.all_gather(mixture_part, "sec"), axis=0)
    return (hidden + mixture).astype(jnp.bfloat16)


def solution(mesh):
    return jax.shard_map(
        shards,
        mesh=mesh,
        in_specs=(
            P("dev", "sec"),
            P(None, "dev", "sec"),
            P(None, "dev", None, "sec"),
            P("dev"),
            P(None, "dev"),
            P("sec", "dev"),
            P("dev"),
            P(),
            P(),
            P("dev", None, "sec"),
            P("dev", None, "sec"),
            P("dev", "sec", None),
        ),
        out_specs=P(None, "dev"),
        check_vma=False,
    )
```

```python
import math

import jax
import jax.numpy as jnp
from jax import lax
from jax.experimental import pallas as pl
from jax.experimental.pallas import tpu as pltpu
from jax.sharding import PartitionSpec as P

D = 4096
QUERY_HEADS = 64
KEY_VALUE_HEADS = 4
HEAD_SIZE = 128
CAP = 64
GROUPS = 32
CHUNKS = 4
CORE_SWAP = [(0, 1), (1, 0), (2, 3), (3, 2)]


def attend_kernel(
    lengths_hbm,
    queries_hbm,
    fresh_hbm,
    gain_hbm,
    cache_ref,
    block_ref,
    lengths_ref,
    queries_ref,
    fresh_ref,
    gain_ref,
    keys,
    values,
    head_queries,
    head_scores,
    head_outputs,
    staged,
    small_sems,
    key_sems,
    value_sems,
    block_sems,
):
    rows = queries_ref.shape[0]
    heads = queries_ref.shape[1] // HEAD_SIZE
    slots = keys.shape[1]
    scale = 1.0 / math.sqrt(HEAD_SIZE)
    key_copies = [
        pltpu.make_async_copy(cache_ref.at[0, r], keys.at[r], key_sems.at[r]) for r in range(rows)
    ]
    value_copies = [
        pltpu.make_async_copy(cache_ref.at[1, r], values.at[r], value_sems.at[r])
        for r in range(rows)
    ]
    small_copies = [
        pltpu.make_async_copy(source, target, small_sems.at[i])
        for i, (source, target) in enumerate(
            (
                (queries_hbm, queries_ref),
                (gain_hbm, gain_ref),
                (fresh_hbm, fresh_ref),
                (lengths_hbm, lengths_ref),
            )
        )
    ]
    for copy in small_copies + key_copies + value_copies:
        copy.start()
    for copy in small_copies:
        copy.wait()
    gain = gain_ref[...]
    high = gain.astype(jnp.bfloat16).astype(jnp.float32)
    middle = (gain - high).astype(jnp.bfloat16).astype(jnp.float32)
    low = gain - high - middle
    place = lax.broadcasted_iota(jnp.int32, (rows, HEAD_SIZE), 0)
    terms = jnp.where(
        place == 0, high, jnp.where(place == 1, middle, jnp.where(place == 2, low, 0.0))
    )
    staged[:, heads * HEAD_SIZE :] = terms.astype(jnp.bfloat16)
    for h in range(heads):
        head_queries[pl.ds(h, rows, stride=heads), :] = queries_ref[
            :, h * HEAD_SIZE : (h + 1) * HEAD_SIZE
        ].astype(jnp.float32)
    for r in range(rows):
        key_copies[r].wait()
        head_scores[r * heads : (r + 1) * heads, :] = lax.dot_general(
            head_queries[r * heads : (r + 1) * heads, :].astype(jnp.bfloat16),
            keys[r],
            (((1,), (1,)), ((), ())),
            preferred_element_type=jnp.float32,
        )
    slot = lax.broadcasted_iota(jnp.int32, (heads, slots), 1)
    weights, own_weights, normalizers = [], [], []
    for r in range(rows):
        own_key = fresh_ref[0, r : r + 1, :].astype(jnp.float32)
        own_score = (
            jnp.sum(
                head_queries[r * heads : (r + 1) * heads, :] * own_key, axis=1, keepdims=True
            )
            * scale
        )
        scores = jnp.where(
            slot < lengths_ref[r], head_scores[r * heads : (r + 1) * heads, :] * scale, -jnp.inf
        )
        row_max = jnp.maximum(jnp.max(scores, axis=1, keepdims=True), own_score)
        weight = jnp.exp(scores - row_max)
        own_weight = jnp.exp(own_score - row_max)
        normalizers.append(jnp.sum(weight, axis=1, keepdims=True) + own_weight)
        weights.append(weight.astype(jnp.bfloat16))
        own_weights.append(own_weight)
    for r in range(rows):
        value_copies[r].wait()
        own_value = fresh_ref[1, r : r + 1, :].astype(jnp.float32)
        weighted = jnp.dot(weights[r], values[r], preferred_element_type=jnp.float32)
        head_outputs[r * heads : (r + 1) * heads, :] = (
            weighted + own_weights[r] * own_value
        ) / normalizers[r]
    for h in range(heads):
        staged[:, h * HEAD_SIZE : (h + 1) * HEAD_SIZE] = head_outputs[
            pl.ds(h, rows, stride=heads), :
        ].astype(jnp.bfloat16)
    block_copies = [
        pltpu.make_async_copy(staged, block_ref.at[i], block_sems.at[i])
        for i in range(block_ref.shape[0])
    ]
    for copy in block_copies:
        copy.start()
    for copy in block_copies:
        copy.wait()


def attend(queries, fresh_key_value, key_value_cache, lengths, norm_gain):
    rows, width = queries.shape
    slots = key_value_cache.shape[2]
    heads = width // HEAD_SIZE
    operands = (lengths, queries, fresh_key_value, norm_gain.reshape(1, HEAD_SIZE), key_value_cache)
    return pl.pallas_call(
        attend_kernel,
        out_shape=jax.ShapeDtypeStruct((GROUPS, rows, width + HEAD_SIZE), jnp.bfloat16),
        in_specs=[pl.BlockSpec(memory_space=pl.ANY)] * len(operands),
        out_specs=pl.BlockSpec(memory_space=pl.ANY),
        scratch_shapes=[
            pltpu.SMEM((rows,), jnp.int32),
            pltpu.VMEM(queries.shape, jnp.bfloat16),
            pltpu.VMEM(fresh_key_value.shape, jnp.bfloat16),
            pltpu.VMEM((1, HEAD_SIZE), jnp.float32),
            pltpu.VMEM((rows, slots, HEAD_SIZE), jnp.bfloat16),
            pltpu.VMEM((rows, slots, HEAD_SIZE), jnp.bfloat16),
            pltpu.VMEM((rows * heads, HEAD_SIZE), jnp.float32),
            pltpu.VMEM((rows * heads, slots), jnp.float32),
            pltpu.VMEM((rows * heads, HEAD_SIZE), jnp.float32),
            pltpu.VMEM((rows, width + HEAD_SIZE), jnp.bfloat16),
            pltpu.SemaphoreType.DMA((4,)),
            pltpu.SemaphoreType.DMA((rows,)),
            pltpu.SemaphoreType.DMA((rows,)),
            pltpu.SemaphoreType.DMA((GROUPS,)),
        ],
        compiler_params=pltpu.CompilerParams(vmem_limit_bytes=12 << 20),
        cost_estimate=pl.CostEstimate(
            flops=4 * rows * heads * slots * HEAD_SIZE,
            bytes_accessed=5 << 20,
            transcendentals=rows * heads * slots,
        ),
        name="attend",
    )(*(pltpu.with_memory_space_constraint(operand, pltpu.HBM) for operand in operands))


def fill_picked(rows_ref, gain_ref, picked):
    groups, cap, width = rows_ref.shape
    square = jnp.zeros((cap, width), jnp.float32)
    for g in range(groups):
        part = rows_ref[g].astype(jnp.float32)
        square = square + part * part
    factor = lax.rsqrt(jnp.sum(square, axis=1, keepdims=True) / D + 1e-06)
    for g in range(groups):
        part = rows_ref[g].astype(jnp.float32)
        picked[:, g * width : (g + 1) * width] = (
            part * factor * gain_ref[g : g + 1, :]
        ).astype(jnp.bfloat16)


def row_copies(source, expert, target, sems):
    count, size = target.shape[0], target.shape[1]
    return [
        pltpu.make_async_copy(
            source.at[expert, pl.ds(k * size, size)], target.at[k], sems.at[k]
        )
        for k in range(count)
    ]


def column_copies(source, expert, target, sems):
    count, size = target.shape[0], target.shape[2]
    return [
        pltpu.make_async_copy(
            source.at[expert, :, pl.ds(k * size, size)], target.at[k], sems.at[k]
        )
        for k in range(count)
    ]


def activate(picked, gate, gate_copies, up, up_copies):
    size = gate.shape[1]
    gate_part = jnp.zeros((CAP, gate.shape[2]), jnp.float32)
    upward = gate_part
    for k in range(gate.shape[0]):
        part = picked[:, k * size : (k + 1) * size]
        gate_copies[k].wait()
        gate_part = gate_part + jnp.dot(part, gate[k], preferred_element_type=jnp.float32)
        up_copies[k].wait()
        upward = upward + jnp.dot(part, up[k], preferred_element_type=jnp.float32)
    return (gate_part / (1.0 + jnp.exp(-gate_part)) * upward).astype(jnp.bfloat16)


def own_expert_kernel(
    rows_ref, gain_ref, share_ref, gate_hbm, up_hbm, down_hbm, out_ref, picked, gate, up, down, sems
):
    expert = lax.rem(lax.axis_index("sec"), 2)
    gate_copies = row_copies(gate_hbm, expert, gate, sems.at[0])
    up_copies = row_copies(up_hbm, expert, up, sems.at[1])
    down_copies = column_copies(down_hbm, expert, down, sems.at[2])
    for gate_copy, up_copy in zip(gate_copies, up_copies):
        gate_copy.start()
        up_copy.start()
    for copy in down_copies:
        copy.start()
    fill_picked(rows_ref, gain_ref, picked)
    activation = activate(picked, gate, gate_copies, up, up_copies)
    share = share_ref[expert]
    step = down.shape[2]
    for k, copy in enumerate(down_copies):
        copy.wait()
        part = jnp.dot(activation, down[k], preferred_element_type=jnp.float32)
        out_ref[:, k * step : (k + 1) * step] = (part * share).astype(jnp.bfloat16)


def other_gate_kernel(rows_ref, gain_ref, gate_hbm, up_hbm, out_ref, picked, gate, up, sems):
    expert = 1 - lax.rem(lax.axis_index("sec"), 2)
    gate_copies = row_copies(gate_hbm, expert, gate, sems.at[0])
    up_copies = row_copies(up_hbm, expert, up, sems.at[1])
    for gate_copy, up_copy in zip(gate_copies, up_copies):
        gate_copy.start()
        up_copy.start()
    fill_picked(rows_ref, gain_ref, picked)
    out_ref[...] = activate(picked, gate, gate_copies, up, up_copies)


def other_down_kernel(activation_ref, moved_ref, share_ref, down_hbm, out_ref, down, sems):
    expert = 1 - lax.rem(lax.axis_index("sec"), 2)
    down_copies = column_copies(down_hbm, expert, down, sems.at[0])
    for copy in down_copies:
        copy.start()
    share = share_ref[expert]
    activation = activation_ref[...]
    width = out_ref.shape[2]
    step = down.shape[2]
    for k, copy in enumerate(down_copies):
        copy.wait()
        part = jnp.dot(activation, down[k], preferred_element_type=jnp.float32)
        part = part * share + moved_ref[:, k * step : (k + 1) * step].astype(jnp.float32)
        for g in range(step // width):
            out_ref[k * step // width + g] = part[:, g * width : (g + 1) * width].astype(
                jnp.bfloat16
            )


def expert_call(kernel, name, out_shape, scratch, small, weights):
    vmem = pl.BlockSpec(memory_space=pltpu.VMEM)
    any_space = pl.BlockSpec(memory_space=pl.ANY)
    size = sum(weight.size // 2 for weight in weights)
    sems = pltpu.SemaphoreType.DMA((len(weights), CHUNKS))
    return pl.pallas_call(
        kernel,
        out_shape=jax.ShapeDtypeStruct(out_shape, jnp.bfloat16),
        in_specs=[vmem] * len(small) + [any_space] * len(weights),
        out_specs=vmem,
        scratch_shapes=[pltpu.VMEM(shape, jnp.bfloat16) for shape in scratch] + [sems],
        compiler_params=pltpu.CompilerParams(vmem_limit_bytes=20 << 20),
        cost_estimate=pl.CostEstimate(
            flops=2 * CAP * size, bytes_accessed=2 * size, transcendentals=0
        ),
        name=name,
    )(
        *(pltpu.with_memory_space_constraint(array, pltpu.VMEM) for array in small),
        *(pltpu.with_memory_space_constraint(array, pltpu.HBM) for array in weights),
    )


def exchange(blocks):
    return lax.all_to_all(blocks, "dev", 0, 0, tiled=True)


def slot_tables(routes):
    expert_ids = jnp.arange(2 * GROUPS, dtype=jnp.int32)
    chosen = jnp.any(routes[:, :, None] == expert_ids, axis=1)
    earlier = jnp.tri(routes.shape[0], k=-1, dtype=jnp.bfloat16)
    rank = jnp.dot(earlier, chosen.astype(jnp.bfloat16), preferred_element_type=jnp.float32)
    return jnp.where(chosen, rank.astype(jnp.int32), -1).T


def one_hot(ranks):
    slot_ids = jnp.arange(CAP, dtype=jnp.int32)[None, :, None]
    return (ranks[:, None, :] == slot_ids).astype(jnp.bfloat16)


def shards(
    queries,
    fresh_key_value,
    key_value_cache,
    lengths,
    residual,
    out_weight,
    norm_gain,
    routes,
    route_weights,
    w_gate,
    w_up,
    w_down,
):
    row_count = routes.shape[0]
    width = queries.shape[1]
    core = lax.axis_index("sec") % 2
    group = lax.axis_index("dev")
    blocks = attend(queries, fresh_key_value, key_value_cache, lengths, norm_gain)
    gathered = exchange(blocks)
    gain = jnp.sum(gathered[:, :3, width:].astype(jnp.float32), axis=1)
    partial_out = jnp.dot(
        gathered[:, :, :width].reshape(row_count, width),
        out_weight,
        preferred_element_type=jnp.float32,
    )
    hidden = residual.astype(jnp.float32) + jnp.sum(lax.all_gather(partial_out, "sec"), axis=0)

    ranks = slot_tables(routes).reshape(GROUPS, 2, row_count)
    own_ranks = lax.dynamic_index_in_dim(ranks, core, 1, keepdims=False)
    other_ranks = lax.dynamic_index_in_dim(ranks, 1 - core, 1, keepdims=False)
    sent = jnp.einsum(
        "ekr,rf->ekf", one_hot(own_ranks), hidden.astype(jnp.bfloat16), preferred_element_type=jnp.float32
    ).astype(jnp.bfloat16)
    own_rows = exchange(sent)
    other_rows = lax.ppermute(own_rows, "sec", CORE_SWAP)

    local_ids = 2 * group + jnp.arange(2, dtype=jnp.int32)
    local_ranks = lax.dynamic_index_in_dim(ranks, group, 0, keepdims=False)
    shares = jnp.sum(
        jnp.where(routes[None] == local_ids[:, None, None], route_weights[None], 0.0), axis=2
    )
    slot_share = jnp.sum(
        jnp.where(
            local_ranks[:, None, :] == jnp.arange(CAP, dtype=jnp.int32)[None, :, None],
            shares[:, None, :],
            0.0,
        ),
        axis=2,
    )

    share = slot_share[:, :, None]
    units = w_gate.shape[2]
    picked_shape = (CAP, D)
    gate_shape = (CHUNKS, D // CHUNKS, units)
    down_shape = (CHUNKS, units, D // CHUNKS)
    own_result = expert_call(
        own_expert_kernel,
        "own_expert",
        (CAP, D),
        [picked_shape, gate_shape, gate_shape, down_shape],
        [own_rows, gain, share],
        [w_gate, w_up, w_down],
    )
    moved = lax.ppermute(own_result, "sec", CORE_SWAP)
    activation = expert_call(
        other_gate_kernel,
        "other_gate",
        (CAP, units),
        [picked_shape, gate_shape, gate_shape],
        [other_rows, gain],
        [w_gate, w_up],
    )
    summed = expert_call(
        other_down_kernel,
        "other_down",
        (GROUPS, CAP, D // GROUPS),
        [down_shape],
        [activation, moved, share],
        [w_down],
    )
    returned = exchange(summed)
    mixture_part = jnp.einsum(
        "ekr,ekf->rf", one_hot(other_ranks), returned, preferred_element_type=jnp.float32
    )
    mixture = jnp.sum(lax.all_gather(mixture_part, "sec"), axis=0)
    return (hidden + mixture).astype(jnp.bfloat16)


def solution(mesh):
    return jax.shard_map(
        shards,
        mesh=mesh,
        in_specs=(
            P("dev", "sec"),
            P(None, "dev", "sec"),
            P(None, "dev", None, "sec"),
            P("dev"),
            P(None, "dev"),
            P("sec", "dev"),
            P("dev"),
            P(),
            P(),
            P("dev", None, "sec"),
            P("dev", None, "sec"),
            P("dev", "sec", None),
        ),
        out_specs=P(None, "dev"),
        check_vma=False,
    )
```

```python
import math

import jax
import jax.numpy as jnp
import numpy as np
from jax import lax
from jax.experimental import pallas as pl
from jax.experimental.pallas import tpu as pltpu
from jax.sharding import PartitionSpec as P

D = 4096
QUERY_HEADS = 64
KEY_VALUE_HEADS = 4
HEAD_SIZE = 128
CAP = 64
GROUPS = 32
PLANE = 16
CHUNKS = 4
ROW_GROUP = 4
AXES = {"y_hi": 2, "core": 2, "z": 4, "y_lo": 2, "x": 4}
SEC = ("y_hi", "core")
DEV = ("z", "y_lo", "x")
SWAP = [(0, 1), (1, 0)]


def attend_kernel(
    lengths_hbm,
    queries_hbm,
    fresh_hbm,
    gain_hbm,
    cache_ref,
    block_ref,
    lengths_ref,
    queries_ref,
    fresh_ref,
    gain_ref,
    keys,
    values,
    head_queries,
    head_scores,
    head_outputs,
    staged,
    small_sems,
    key_sems,
    value_sems,
    block_sems,
):
    rows = queries_ref.shape[0]
    heads = queries_ref.shape[1] // HEAD_SIZE
    slots = keys.shape[1]
    scale = 1.0 / math.sqrt(HEAD_SIZE)
    key_copies = [
        pltpu.make_async_copy(cache_ref.at[0, r], keys.at[r], key_sems.at[r]) for r in range(rows)
    ]
    value_copies = [
        pltpu.make_async_copy(cache_ref.at[1, r], values.at[r], value_sems.at[r])
        for r in range(rows)
    ]
    small_copies = [
        pltpu.make_async_copy(source, target, small_sems.at[i])
        for i, (source, target) in enumerate(
            (
                (queries_hbm, queries_ref),
                (gain_hbm, gain_ref),
                (fresh_hbm, fresh_ref),
                (lengths_hbm, lengths_ref),
            )
        )
    ]
    for copy in small_copies + [c for pair in zip(key_copies, value_copies) for c in pair]:
        copy.start()
    for copy in small_copies:
        copy.wait()
    gain = gain_ref[...]
    high = gain.astype(jnp.bfloat16).astype(jnp.float32)
    middle = (gain - high).astype(jnp.bfloat16).astype(jnp.float32)
    low = gain - high - middle
    place = lax.broadcasted_iota(jnp.int32, (rows, HEAD_SIZE), 0)
    terms = jnp.where(
        place == 0, high, jnp.where(place == 1, middle, jnp.where(place == 2, low, 0.0))
    )
    staged[:, heads * HEAD_SIZE :] = terms.astype(jnp.bfloat16)
    for h in range(heads):
        head_queries[pl.ds(h, rows, stride=heads), :] = queries_ref[
            :, h * HEAD_SIZE : (h + 1) * HEAD_SIZE
        ].astype(jnp.float32)
    slot = lax.broadcasted_iota(jnp.int32, (heads, slots), 1)
    pending = {}

    def score(r):
        return lax.dot_general(
            head_queries[r * heads : (r + 1) * heads, :].astype(jnp.bfloat16),
            keys[r],
            (((1,), (1,)), ((), ())),
            preferred_element_type=jnp.float32,
        )

    def weigh(r, scores):
        own_key = fresh_ref[0, r : r + 1, :].astype(jnp.float32)
        own_score = (
            jnp.sum(
                head_queries[r * heads : (r + 1) * heads, :] * own_key, axis=1, keepdims=True
            )
            * scale
        )
        scores = jnp.where(slot < lengths_ref[r], scores * scale, -jnp.inf)
        row_max = jnp.maximum(jnp.max(scores, axis=1, keepdims=True), own_score)
        weight = jnp.exp(scores - row_max)
        own_weight = jnp.exp(own_score - row_max)
        normalizer = jnp.sum(weight, axis=1, keepdims=True) + own_weight
        return weight.astype(jnp.bfloat16), own_weight, normalizer

    def blend(r, weight, own_weight, normalizer):
        own_value = fresh_ref[1, r : r + 1, :].astype(jnp.float32)
        weighted = jnp.dot(weight, values[r], preferred_element_type=jnp.float32)
        head_outputs[r * heads : (r + 1) * heads, :] = (
            weighted + own_weight * own_value
        ) / normalizer

    scored, weighed = {}, {}
    groups = rows // ROW_GROUP
    members = lambda g: range(g * ROW_GROUP, (g + 1) * ROW_GROUP)
    for g in range(groups + 2):
        if g < groups:
            for r in members(g):
                key_copies[r].wait()
        if g >= 2:
            for r in members(g - 2):
                value_copies[r].wait()
        if g < groups:
            for r in members(g):
                scored[r] = score(r)
        if 1 <= g <= groups:
            for r in members(g - 1):
                weighed[r] = weigh(r, scored.pop(r))
        if g >= 2:
            for r in members(g - 2):
                blend(r, *weighed.pop(r))
    for h in range(heads):
        staged[:, h * HEAD_SIZE : (h + 1) * HEAD_SIZE] = head_outputs[
            pl.ds(h, rows, stride=heads), :
        ].astype(jnp.bfloat16)
    block_copies = [
        pltpu.make_async_copy(staged, block_ref.at[i], block_sems.at[i])
        for i in range(block_ref.shape[0])
    ]
    for copy in block_copies:
        copy.start()
    for copy in block_copies:
        copy.wait()


def attend(queries, fresh_key_value, key_value_cache, lengths, norm_gain):
    rows, width = queries.shape
    slots = key_value_cache.shape[2]
    heads = width // HEAD_SIZE
    operands = (lengths, queries, fresh_key_value, norm_gain.reshape(1, HEAD_SIZE), key_value_cache)
    return pl.pallas_call(
        attend_kernel,
        out_shape=jax.ShapeDtypeStruct((PLANE, rows, width + HEAD_SIZE), jnp.bfloat16),
        in_specs=[pl.BlockSpec(memory_space=pl.ANY)] * len(operands),
        out_specs=pl.BlockSpec(memory_space=pl.ANY),
        scratch_shapes=[
            pltpu.SMEM((rows,), jnp.int32),
            pltpu.VMEM(queries.shape, jnp.bfloat16),
            pltpu.VMEM(fresh_key_value.shape, jnp.bfloat16),
            pltpu.VMEM((1, HEAD_SIZE), jnp.float32),
            pltpu.VMEM((rows, slots, HEAD_SIZE), jnp.bfloat16),
            pltpu.VMEM((rows, slots, HEAD_SIZE), jnp.bfloat16),
            pltpu.VMEM((rows * heads, HEAD_SIZE), jnp.float32),
            pltpu.VMEM((rows * heads, slots), jnp.float32),
            pltpu.VMEM((rows * heads, HEAD_SIZE), jnp.float32),
            pltpu.VMEM((rows, width + HEAD_SIZE), jnp.bfloat16),
            pltpu.SemaphoreType.DMA((4,)),
            pltpu.SemaphoreType.DMA((rows,)),
            pltpu.SemaphoreType.DMA((rows,)),
            pltpu.SemaphoreType.DMA((PLANE,)),
        ],
        compiler_params=pltpu.CompilerParams(vmem_limit_bytes=12 << 20),
        cost_estimate=pl.CostEstimate(
            flops=4 * rows * heads * slots * HEAD_SIZE,
            bytes_accessed=5 << 20,
            transcendentals=rows * heads * slots,
        ),
        name="attend",
    )(*(pltpu.with_memory_space_constraint(operand, pltpu.HBM) for operand in operands))


def fill_picked(rows_ref, gain_ref, picked):
    groups, cap, width = rows_ref.shape
    square = jnp.zeros((cap, width), jnp.float32)
    for g in range(groups):
        part = rows_ref[g].astype(jnp.float32)
        square = square + part * part
    factor = lax.rsqrt(jnp.sum(square, axis=1, keepdims=True) / D + 1e-06)
    for g in range(groups):
        part = rows_ref[g].astype(jnp.float32)
        picked[:, g * width : (g + 1) * width] = (
            part * factor * gain_ref[g : g + 1, :]
        ).astype(jnp.bfloat16)


def row_copies(source, expert, target, sems):
    count, size = target.shape[0], target.shape[1]
    return [
        pltpu.make_async_copy(
            source.at[expert, pl.ds(k * size, size)], target.at[k], sems.at[k]
        )
        for k in range(count)
    ]


def column_copies(source, expert, target, sems):
    count, size = target.shape[0], target.shape[2]
    return [
        pltpu.make_async_copy(
            source.at[expert, :, pl.ds(k * size, size)], target.at[k], sems.at[k]
        )
        for k in range(count)
    ]


def activate(picked, gate, gate_copies, up, up_copies):
    size = gate.shape[1]
    gate_part = jnp.zeros((CAP, gate.shape[2]), jnp.float32)
    upward = gate_part
    for k in range(gate.shape[0]):
        part = picked[:, k * size : (k + 1) * size]
        gate_copies[k].wait()
        gate_part = gate_part + jnp.dot(part, gate[k], preferred_element_type=jnp.float32)
        up_copies[k].wait()
        upward = upward + jnp.dot(part, up[k], preferred_element_type=jnp.float32)
    return (gate_part / (1.0 + jnp.exp(-gate_part)) * upward).astype(jnp.bfloat16)


def own_expert_kernel(
    rows_ref,
    gain_ref,
    share_ref,
    gate_hbm,
    up_hbm,
    down_hbm,
    out_ref,
    next_down,
    picked,
    gate,
    up,
    down,
    sems,
):
    expert = lax.axis_index("core")
    gate_copies = row_copies(gate_hbm, expert, gate, sems.at[0])
    up_copies = row_copies(up_hbm, expert, up, sems.at[1])
    down_copies = column_copies(down_hbm, expert, down, sems.at[2])
    next_copies = column_copies(down_hbm, 1 - expert, next_down, sems.at[3])
    for gate_copy, up_copy in zip(gate_copies, up_copies):
        gate_copy.start()
        up_copy.start()
    for copy in down_copies + next_copies:
        copy.start()
    fill_picked(rows_ref, gain_ref, picked)
    activation = activate(picked, gate, gate_copies, up, up_copies)
    share = share_ref[expert]
    step = down.shape[2]
    for k, copy in enumerate(down_copies):
        copy.wait()
        part = jnp.dot(activation, down[k], preferred_element_type=jnp.float32)
        out_ref[:, k * step : (k + 1) * step] = (part * share).astype(jnp.bfloat16)
    for copy in next_copies:
        copy.wait()


def other_gate_kernel(rows_ref, gain_ref, gate_hbm, up_hbm, out_ref, picked, gate, up, sems):
    expert = 1 - lax.axis_index("core")
    gate_copies = row_copies(gate_hbm, expert, gate, sems.at[0])
    up_copies = row_copies(up_hbm, expert, up, sems.at[1])
    for gate_copy, up_copy in zip(gate_copies, up_copies):
        gate_copy.start()
        up_copy.start()
    fill_picked(rows_ref, gain_ref, picked)
    out_ref[...] = activate(picked, gate, gate_copies, up, up_copies)


def other_down_kernel(activation_ref, moved_ref, share_ref, down, out_hbm, staged, sems):
    expert = 1 - lax.axis_index("core")
    share = share_ref[expert]
    activation = activation_ref[...]
    width = staged.shape[2]
    step = down.shape[2]
    groups = step // width
    copies = []
    for k in range(down.shape[0]):
        part = jnp.dot(activation, down[k], preferred_element_type=jnp.float32)
        part = part * share + moved_ref[:, k * step : (k + 1) * step].astype(jnp.float32)
        for g in range(groups):
            staged[k * groups + g] = part[:, g * width : (g + 1) * width].astype(jnp.bfloat16)
        place = pl.ds(k * groups, groups)
        copies.append(pltpu.make_async_copy(staged.at[place], out_hbm.at[place], sems.at[0, k]))
        copies[-1].start()
    for copy in copies:
        copy.wait()


def expert_call(kernel, name, outs, scratch, small, weights):
    vmem = pl.BlockSpec(memory_space=pltpu.VMEM)
    any_space = pl.BlockSpec(memory_space=pl.ANY)
    size = sum(weight.size // 2 for weight in weights)
    return pl.pallas_call(
        kernel,
        out_shape=[space(shape, jnp.bfloat16) for space, shape in outs],
        in_specs=[vmem] * len(small) + [any_space] * len(weights),
        out_specs=[vmem if space is pltpu.VMEM else any_space for space, _ in outs],
        scratch_shapes=[pltpu.VMEM(shape, jnp.bfloat16) for shape in scratch]
        + [pltpu.SemaphoreType.DMA((4, CHUNKS))],
        compiler_params=pltpu.CompilerParams(vmem_limit_bytes=20 << 20),
        cost_estimate=pl.CostEstimate(
            flops=2 * CAP * size, bytes_accessed=2 * size, transcendentals=0
        ),
        name=name,
    )(
        *(pltpu.with_memory_space_constraint(array, pltpu.VMEM) for array in small),
        *(pltpu.with_memory_space_constraint(array, pltpu.HBM) for array in weights),
    )


def exchange(blocks, axes):
    return lax.all_to_all(blocks, axes, 0, 0, tiled=True)


def project_kernel(gathered_ref, own_ref, pair_ref, out_ref):
    half = lax.axis_index("y_lo")
    rows, width = out_ref.shape[1], own_ref.shape[0]
    attn = gathered_ref[:, :, :width].reshape(rows, width)
    own = jnp.dot(attn, own_ref[...], preferred_element_type=jnp.float32).astype(jnp.bfloat16)
    pair = jnp.dot(attn, pair_ref[...], preferred_element_type=jnp.float32).astype(jnp.bfloat16)
    for s in range(out_ref.shape[0] // 2):
        out_ref[2 * s + half] = own
        out_ref[2 * s + 1 - half] = pair


def project(gathered, own, pair):
    vmem = pl.BlockSpec(memory_space=pltpu.VMEM)
    groups, rows, _ = gathered.shape
    width, features = own.shape
    return pl.pallas_call(
        project_kernel,
        out_shape=jax.ShapeDtypeStruct((8, groups * rows, features), jnp.bfloat16),
        in_specs=[vmem] * 3,
        out_specs=vmem,
        compiler_params=pltpu.CompilerParams(vmem_limit_bytes=8 << 20),
        cost_estimate=pl.CostEstimate(
            flops=4 * groups * rows * own.size, bytes_accessed=2 << 20, transcendentals=0
        ),
        name="project",
    )(gathered, own, pair)


def dispatch_kernel(parts_ref, residual_ref, ranks_ref, hidden_ref, sent_ref, mask):
    rows, features = residual_ref.shape
    span = parts_ref.shape[1] // AXES["z"]
    for z in range(AXES["z"]):
        for half in range(2):
            place = (2 * z + half) * span
            total = residual_ref[place : place + span, :].astype(jnp.float32)
            for s in range(4):
                part = parts_ref[2 * s + half, z * span : (z + 1) * span, :]
                total = total + part.astype(jnp.float32)
            hidden_ref[place : place + span, :] = total
    slot = lax.broadcasted_iota(jnp.int32, (CAP, rows), 0)
    for e in range(GROUPS):
        mask[e * CAP : (e + 1) * CAP, :] = jnp.where(
            ranks_ref[e : e + 1, :] == slot, 1.0, 0.0
        ).astype(jnp.bfloat16)
    hidden = hidden_ref[...].astype(jnp.bfloat16)
    step = 8
    for e in range(0, GROUPS, step):
        picked = jnp.dot(
            mask[e * CAP : (e + step) * CAP, :], hidden, preferred_element_type=jnp.float32
        ).astype(jnp.bfloat16)
        for i in range(step):
            sent_ref[e + i] = picked[i * CAP : (i + 1) * CAP, :]


def dispatch(parts, residual, ranks):
    vmem = pl.BlockSpec(memory_space=pltpu.VMEM)
    rows, features = residual.shape
    return pl.pallas_call(
        dispatch_kernel,
        out_shape=[
            jax.ShapeDtypeStruct((rows, features), jnp.float32),
            jax.ShapeDtypeStruct((GROUPS, CAP, features), jnp.bfloat16),
        ],
        in_specs=[vmem] * 3,
        out_specs=[vmem] * 2,
        scratch_shapes=[pltpu.VMEM((GROUPS * CAP, rows), jnp.bfloat16)],
        compiler_params=pltpu.CompilerParams(vmem_limit_bytes=8 << 20),
        cost_estimate=pl.CostEstimate(
            flops=2 * GROUPS * CAP * rows * features, bytes_accessed=2 << 20, transcendentals=0
        ),
        name="dispatch",
    )(parts, residual, ranks)


def sum_over_sec(part):
    pair = part + lax.ppermute(part, "core", SWAP)
    pair = pair.astype(jnp.bfloat16)
    return pair.astype(jnp.float32) + lax.ppermute(pair, "y_hi", SWAP).astype(jnp.float32)


def slot_tables(routes):
    expert_ids = jnp.arange(2 * GROUPS, dtype=jnp.int32)
    chosen = jnp.any(routes[:, :, None] == expert_ids, axis=1)
    earlier = jnp.tri(routes.shape[0], k=-1, dtype=jnp.bfloat16)
    rank = jnp.dot(earlier, chosen.astype(jnp.bfloat16), preferred_element_type=jnp.float32)
    return jnp.where(chosen, rank.astype(jnp.int32), -1).T


def one_hot(ranks):
    slot_ids = jnp.arange(CAP, dtype=jnp.int32)[None, :, None]
    return (ranks[:, None, :] == slot_ids).astype(jnp.bfloat16)


def shards(
    queries,
    fresh_key_value,
    key_value_cache,
    lengths,
    residual,
    out_weight,
    norm_gain,
    routes,
    route_weights,
    w_gate,
    w_up,
    w_down,
):
    row_count = routes.shape[0]
    width = queries.shape[1]
    core = lax.axis_index("core")
    half = lax.axis_index("y_lo")
    group = lax.axis_index(DEV)
    pair_weight = lax.ppermute(out_weight, "y_lo", SWAP)
    blocks = attend(queries, fresh_key_value, key_value_cache, lengths, norm_gain)
    gathered = exchange(blocks, ("z", "x"))
    parts = exchange(project(gathered, out_weight, pair_weight), ("y_hi", "core", "y_lo"))
    own_gain = jnp.sum(gathered[:, :3, width:].astype(jnp.float32), axis=1)
    pair_gain = lax.ppermute(own_gain, "y_lo", SWAP)
    gain = jnp.where(half == 0, jnp.stack([own_gain, pair_gain]), jnp.stack([pair_gain, own_gain]))
    gain = gain.reshape(2, AXES["z"], AXES["x"], HEAD_SIZE).transpose(1, 0, 2, 3)
    gain = gain.reshape(GROUPS, HEAD_SIZE)

    ranks = slot_tables(routes).reshape(GROUPS, 2, row_count)
    own_ranks = lax.dynamic_index_in_dim(ranks, core, 1, keepdims=False)
    other_ranks = lax.dynamic_index_in_dim(ranks, 1 - core, 1, keepdims=False)
    hidden, sent = dispatch(parts, residual, own_ranks)
    own_rows = exchange(sent, DEV)
    other_rows = lax.ppermute(own_rows, "core", SWAP)

    local_ids = 2 * group + jnp.arange(2, dtype=jnp.int32)
    local_ranks = lax.dynamic_index_in_dim(ranks, group, 0, keepdims=False)
    shares = jnp.sum(
        jnp.where(routes[None] == local_ids[:, None, None], route_weights[None], 0.0), axis=2
    )
    slot_share = jnp.sum(
        jnp.where(
            local_ranks[:, None, :] == jnp.arange(CAP, dtype=jnp.int32)[None, :, None],
            shares[:, None, :],
            0.0,
        ),
        axis=2,
    )

    share = slot_share[:, :, None]
    units = w_gate.shape[2]
    picked_shape = (CAP, D)
    gate_shape = (CHUNKS, D // CHUNKS, units)
    down_shape = (CHUNKS, units, D // CHUNKS)
    own_result, next_down = expert_call(
        own_expert_kernel,
        "own_expert",
        [(pltpu.VMEM, (CAP, D)), (pltpu.VMEM, down_shape)],
        [picked_shape, gate_shape, gate_shape, down_shape],
        [own_rows, gain, share],
        [w_gate, w_up, w_down],
    )
    moved = lax.ppermute(own_result, "core", SWAP)
    (activation,) = expert_call(
        other_gate_kernel,
        "other_gate",
        [(pltpu.VMEM, (CAP, units))],
        [picked_shape, gate_shape, gate_shape],
        [other_rows, gain],
        [w_gate, w_up],
    )
    out_shape = (GROUPS, CAP, D // GROUPS)
    (summed,) = expert_call(
        other_down_kernel,
        "other_down",
        [(pltpu.HBM, out_shape)],
        [out_shape],
        [activation, moved, share, next_down],
        [],
    )
    returned = exchange(summed, DEV)
    mixture_part = jnp.einsum(
        "ekr,ekf->rf", one_hot(other_ranks), returned, preferred_element_type=jnp.float32
    )
    mixture = sum_over_sec(mixture_part)
    return (hidden + mixture).astype(jnp.bfloat16)


def solution(mesh):
    named = jax.sharding.Mesh(
        np.reshape(mesh.devices, tuple(AXES.values())), tuple(AXES)
    )
    return jax.shard_map(
        shards,
        mesh=named,
        in_specs=(
            P(DEV, SEC),
            P(None, DEV, SEC),
            P(None, DEV, None, SEC),
            P(DEV),
            P(None, DEV),
            P(SEC, DEV),
            P(DEV),
            P(),
            P(),
            P(DEV, None, SEC),
            P(DEV, None, SEC),
            P(DEV, SEC, None),
        ),
        out_specs=P(None, DEV),
        check_vma=False,
    )
```

```python
import functools
import math

import jax
import jax.numpy as jnp
import numpy as np
from jax import lax
from jax.experimental import pallas as pl
from jax.experimental.pallas import tpu as pltpu
from jax.sharding import PartitionSpec as P

D = 4096
QUERY_HEADS = 64
KEY_VALUE_HEADS = 4
HEAD_SIZE = 128
CAP = 64
GROUPS = 32
PLANE = 16
GATE_CHUNKS = 4
FIRST = 1536
DOWN_CHUNKS = 4
ROW_GROUP = 4
AXES = {"y_hi": 2, "core": 2, "z": 4, "y_lo": 2, "x": 4}
SEC = ("y_hi", "core")
DEV = ("z", "y_lo", "x")
SWAP = [(0, 1), (1, 0)]


def attend_kernel(
    lengths_hbm,
    queries_hbm,
    fresh_hbm,
    gain_hbm,
    cache_ref,
    block_ref,
    lengths_ref,
    queries_ref,
    fresh_ref,
    gain_ref,
    keys,
    values,
    head_queries,
    head_scores,
    head_outputs,
    staged,
    small_sems,
    key_sems,
    value_sems,
    block_sems,
):
    rows = queries_ref.shape[0]
    heads = queries_ref.shape[1] // HEAD_SIZE
    slots = keys.shape[1]
    scale = 1.0 / math.sqrt(HEAD_SIZE)
    key_copies = [
        pltpu.make_async_copy(cache_ref.at[0, r], keys.at[r], key_sems.at[r]) for r in range(rows)
    ]
    value_copies = [
        pltpu.make_async_copy(cache_ref.at[1, r], values.at[r], value_sems.at[r])
        for r in range(rows)
    ]
    small_copies = [
        pltpu.make_async_copy(source, target, small_sems.at[i])
        for i, (source, target) in enumerate(
            (
                (queries_hbm, queries_ref),
                (gain_hbm, gain_ref),
                (fresh_hbm, fresh_ref),
                (lengths_hbm, lengths_ref),
            )
        )
    ]
    for copy in small_copies + [c for pair in zip(key_copies, value_copies) for c in pair]:
        copy.start()
    for copy in small_copies:
        copy.wait()
    gain = gain_ref[...]
    high = gain.astype(jnp.bfloat16).astype(jnp.float32)
    middle = (gain - high).astype(jnp.bfloat16).astype(jnp.float32)
    low = gain - high - middle
    place = lax.broadcasted_iota(jnp.int32, (rows, HEAD_SIZE), 0)
    terms = jnp.where(
        place == 0, high, jnp.where(place == 1, middle, jnp.where(place == 2, low, 0.0))
    )
    staged[:, heads * HEAD_SIZE :] = terms.astype(jnp.bfloat16)
    for h in range(heads):
        head_queries[pl.ds(h, rows, stride=heads), :] = queries_ref[
            :, h * HEAD_SIZE : (h + 1) * HEAD_SIZE
        ].astype(jnp.float32)
    slot = lax.broadcasted_iota(jnp.int32, (heads, slots), 1)
    pending = {}

    def score(r):
        return lax.dot_general(
            head_queries[r * heads : (r + 1) * heads, :].astype(jnp.bfloat16),
            keys[r],
            (((1,), (1,)), ((), ())),
            preferred_element_type=jnp.float32,
        )

    def weigh(r, scores):
        own_key = fresh_ref[0, r : r + 1, :].astype(jnp.float32)
        own_score = (
            jnp.sum(
                head_queries[r * heads : (r + 1) * heads, :] * own_key, axis=1, keepdims=True
            )
            * scale
        )
        scores = jnp.where(slot < lengths_ref[r], scores * scale, -jnp.inf)
        row_max = jnp.maximum(jnp.max(scores, axis=1, keepdims=True), own_score)
        weight = jnp.exp(scores - row_max)
        own_weight = jnp.exp(own_score - row_max)
        normalizer = jnp.sum(weight, axis=1, keepdims=True) + own_weight
        return weight.astype(jnp.bfloat16), own_weight, normalizer

    def blend(r, weight, own_weight, normalizer):
        own_value = fresh_ref[1, r : r + 1, :].astype(jnp.float32)
        weighted = jnp.dot(weight, values[r], preferred_element_type=jnp.float32)
        head_outputs[r * heads : (r + 1) * heads, :] = (
            weighted + own_weight * own_value
        ) / normalizer

    scored, weighed = {}, {}
    groups = rows // ROW_GROUP
    members = lambda g: range(g * ROW_GROUP, (g + 1) * ROW_GROUP)
    for g in range(groups + 2):
        if g < groups:
            for r in members(g):
                key_copies[r].wait()
        if g >= 2:
            for r in members(g - 2):
                value_copies[r].wait()
        if g < groups:
            for r in members(g):
                scored[r] = score(r)
        if 1 <= g <= groups:
            for r in members(g - 1):
                weighed[r] = weigh(r, scored.pop(r))
        if g >= 2:
            for r in members(g - 2):
                blend(r, *weighed.pop(r))
    for h in range(heads):
        staged[:, h * HEAD_SIZE : (h + 1) * HEAD_SIZE] = head_outputs[
            pl.ds(h, rows, stride=heads), :
        ].astype(jnp.bfloat16)
    block_copies = [
        pltpu.make_async_copy(staged, block_ref.at[i], block_sems.at[i])
        for i in range(block_ref.shape[0])
    ]
    for copy in block_copies:
        copy.start()
    for copy in block_copies:
        copy.wait()


def attend(queries, fresh_key_value, key_value_cache, lengths, norm_gain):
    rows, width = queries.shape
    slots = key_value_cache.shape[2]
    heads = width // HEAD_SIZE
    operands = (lengths, queries, fresh_key_value, norm_gain.reshape(1, HEAD_SIZE), key_value_cache)
    return pl.pallas_call(
        attend_kernel,
        out_shape=jax.ShapeDtypeStruct((PLANE, rows, width + HEAD_SIZE), jnp.bfloat16),
        in_specs=[pl.BlockSpec(memory_space=pl.ANY)] * len(operands),
        out_specs=pl.BlockSpec(memory_space=pl.ANY),
        scratch_shapes=[
            pltpu.SMEM((rows,), jnp.int32),
            pltpu.VMEM(queries.shape, jnp.bfloat16),
            pltpu.VMEM(fresh_key_value.shape, jnp.bfloat16),
            pltpu.VMEM((1, HEAD_SIZE), jnp.float32),
            pltpu.VMEM((rows, slots, HEAD_SIZE), jnp.bfloat16),
            pltpu.VMEM((rows, slots, HEAD_SIZE), jnp.bfloat16),
            pltpu.VMEM((rows * heads, HEAD_SIZE), jnp.float32),
            pltpu.VMEM((rows * heads, slots), jnp.float32),
            pltpu.VMEM((rows * heads, HEAD_SIZE), jnp.float32),
            pltpu.VMEM((rows, width + HEAD_SIZE), jnp.bfloat16),
            pltpu.SemaphoreType.DMA((4,)),
            pltpu.SemaphoreType.DMA((rows,)),
            pltpu.SemaphoreType.DMA((rows,)),
            pltpu.SemaphoreType.DMA((PLANE,)),
        ],
        compiler_params=pltpu.CompilerParams(vmem_limit_bytes=12 << 20),
        cost_estimate=pl.CostEstimate(
            flops=4 * rows * heads * slots * HEAD_SIZE,
            bytes_accessed=5 << 20,
            transcendentals=rows * heads * slots,
        ),
        name="attend",
    )(*(pltpu.with_memory_space_constraint(operand, pltpu.HBM) for operand in operands))


def land(copies):
    for copy in copies:
        copy.wait()
        yield


def in_order(copies, meanwhile):
    for copy in copies:
        copy.start()
    meanwhile()
    return land(copies)


def fill_picked(rows_ref, gain_ref, picked):
    groups, cap, width = rows_ref.shape
    square = jnp.zeros((cap, width), jnp.float32)
    for g in range(groups):
        part = rows_ref[g].astype(jnp.float32)
        square = square + part * part
    factor = lax.rsqrt(jnp.sum(square, axis=1, keepdims=True) / D + 1e-06)
    for g in range(groups):
        part = rows_ref[g].astype(jnp.float32)
        picked[:, g * width : (g + 1) * width] = (
            part * factor * gain_ref[g : g + 1, :]
        ).astype(jnp.bfloat16)


def row_copies(source, expert, target, sems, skipped=0):
    count, size = target.shape[0], target.shape[1]
    return [
        pltpu.make_async_copy(
            source.at[expert, pl.ds(skipped + k * size, size)], target.at[k], sems.at[k]
        )
        for k in range(count)
    ]


def column_copies(source, expert, target, sems):
    count, size = target.shape[0], target.shape[2]
    return [
        pltpu.make_async_copy(
            source.at[expert, :, pl.ds(k * size, size)], target.at[k], sems.at[k]
        )
        for k in range(count)
    ]


def activate(picked, gates, ups, landed, skipped):
    gate_sum = up_sum = None
    start = 0
    for k, (gate, up) in enumerate(zip(gates, ups)):
        part = picked[:, start : start + gate.shape[0]]
        start += gate.shape[0]
        if k >= skipped:
            next(landed)
        product = jnp.dot(part, gate[...], preferred_element_type=jnp.float32)
        gate_sum = product if gate_sum is None else gate_sum + product
        if k >= skipped:
            next(landed)
        product = jnp.dot(part, up[...], preferred_element_type=jnp.float32)
        up_sum = product if up_sum is None else up_sum + product
    return (gate_sum / (1.0 + jnp.exp(-gate_sum)) * up_sum).astype(jnp.bfloat16)


def parts_of(array):
    return [array.at[k] for k in range(array.shape[0])]


def paired(first, second):
    return [copy for pair in zip(first, second) for copy in pair]


def preload_kernel(gate_hbm, up_hbm, gate_ref, up_ref, sems):
    expert = lax.axis_index("core")
    place = pl.ds(0, gate_ref.shape[0])
    copies = [
        pltpu.make_async_copy(gate_hbm.at[expert, place], gate_ref, sems.at[0]),
        pltpu.make_async_copy(up_hbm.at[expert, place], up_ref, sems.at[1]),
    ]
    for copy in copies:
        copy.start()
    for copy in copies:
        copy.wait()


def preload(gate, up, rows):
    shape = (rows, gate.shape[2])
    return pl.pallas_call(
        preload_kernel,
        out_shape=[pltpu.VMEM(shape, jnp.bfloat16)] * 2,
        in_specs=[pl.BlockSpec(memory_space=pl.ANY)] * 2,
        out_specs=[pl.BlockSpec(memory_space=pltpu.VMEM)] * 2,
        scratch_shapes=[pltpu.SemaphoreType.DMA((2,))],
        compiler_params=pltpu.CompilerParams(vmem_limit_bytes=1 << 20),
        cost_estimate=pl.CostEstimate(
            flops=0, bytes_accessed=8 * rows * gate.shape[2], transcendentals=0
        ),
        name="preload",
    )(
        pltpu.with_memory_space_constraint(gate, pltpu.HBM),
        pltpu.with_memory_space_constraint(up, pltpu.HBM),
    )


def own_expert_kernel(
    rows_ref,
    gain_ref,
    share_ref,
    first_gate,
    first_up,
    gate_hbm,
    up_hbm,
    down_hbm,
    out_ref,
    next_down,
    picked,
    gate,
    up,
    down,
    sems,
):
    expert = lax.axis_index("core")
    skipped = first_gate.shape[0]
    gate_copies = row_copies(gate_hbm, expert, gate, sems.at[0], skipped)
    up_copies = row_copies(up_hbm, expert, up, sems.at[1], skipped)
    down_copies = column_copies(down_hbm, expert, down, sems.at[2])
    next_copies = column_copies(down_hbm, 1 - expert, next_down, sems.at[3])
    copies = paired(gate_copies, up_copies) + down_copies + next_copies
    landed = in_order(copies, functools.partial(fill_picked, rows_ref, gain_ref, picked))
    activation = activate(
        picked, [first_gate] + parts_of(gate), [first_up] + parts_of(up), landed, 1
    )
    share = share_ref[expert]
    step = down.shape[2]
    for k in range(down.shape[0]):
        next(landed)
        part = jnp.dot(activation, down[k], preferred_element_type=jnp.float32)
        out_ref[:, k * step : (k + 1) * step] = (part * share).astype(jnp.bfloat16)
    for _ in landed:
        pass


def other_gate_kernel(rows_ref, gain_ref, gate_hbm, up_hbm, out_ref, picked, gate, up, sems):
    expert = 1 - lax.axis_index("core")
    gate_copies = row_copies(gate_hbm, expert, gate, sems.at[0])
    up_copies = row_copies(up_hbm, expert, up, sems.at[1])
    landed = in_order(
        paired(gate_copies, up_copies), functools.partial(fill_picked, rows_ref, gain_ref, picked)
    )
    out_ref[...] = activate(picked, parts_of(gate), parts_of(up), landed, 0)
    for _ in landed:
        pass


def other_down_kernel(activation_ref, moved_ref, share_ref, down, out_hbm, staged, sems):
    expert = 1 - lax.axis_index("core")
    share = share_ref[expert]
    activation = activation_ref[...]
    width = staged.shape[2]
    step = down.shape[2]
    groups = step // width
    copies = []
    for k in range(down.shape[0]):
        part = jnp.dot(activation, down[k], preferred_element_type=jnp.float32)
        part = part * share + moved_ref[:, k * step : (k + 1) * step].astype(jnp.float32)
        for g in range(groups):
            staged[k * groups + g] = part[:, g * width : (g + 1) * width].astype(jnp.bfloat16)
        place = pl.ds(k * groups, groups)
        copies.append(pltpu.make_async_copy(staged.at[place], out_hbm.at[place], sems.at[0, k]))
        copies[-1].start()
    for copy in copies:
        copy.wait()


def expert_call(kernel, name, outs, scratch, small, weights):
    vmem = pl.BlockSpec(memory_space=pltpu.VMEM)
    any_space = pl.BlockSpec(memory_space=pl.ANY)
    size = sum(weight.size // 2 for weight in weights)
    return pl.pallas_call(
        kernel,
        out_shape=[space(shape, jnp.bfloat16) for space, shape in outs],
        in_specs=[vmem] * len(small) + [any_space] * len(weights),
        out_specs=[vmem if space is pltpu.VMEM else any_space for space, _ in outs],
        scratch_shapes=[pltpu.VMEM(shape, jnp.bfloat16) for shape in scratch]
        + [pltpu.SemaphoreType.DMA((4, max(GATE_CHUNKS, DOWN_CHUNKS)))],
        compiler_params=pltpu.CompilerParams(vmem_limit_bytes=16 << 20),
        cost_estimate=pl.CostEstimate(
            flops=2 * CAP * size, bytes_accessed=2 * size, transcendentals=0
        ),
        name=name,
    )(
        *(pltpu.with_memory_space_constraint(array, pltpu.VMEM) for array in small),
        *(pltpu.with_memory_space_constraint(array, pltpu.HBM) for array in weights),
    )


def exchange(blocks, axes):
    return lax.all_to_all(blocks, axes, 0, 0, tiled=True)


def project_kernel(gathered_ref, own_ref, pair_ref, out_ref):
    half = lax.axis_index("y_lo")
    rows, width = out_ref.shape[1], own_ref.shape[0]
    attn = gathered_ref[:, :, :width].reshape(rows, width)
    own = jnp.dot(attn, own_ref[...], preferred_element_type=jnp.float32).astype(jnp.bfloat16)
    pair = jnp.dot(attn, pair_ref[...], preferred_element_type=jnp.float32).astype(jnp.bfloat16)
    for s in range(out_ref.shape[0] // 2):
        out_ref[2 * s + half] = own
        out_ref[2 * s + 1 - half] = pair


def project(gathered, own, pair):
    vmem = pl.BlockSpec(memory_space=pltpu.VMEM)
    groups, rows, _ = gathered.shape
    width, features = own.shape
    return pl.pallas_call(
        project_kernel,
        out_shape=jax.ShapeDtypeStruct((8, groups * rows, features), jnp.bfloat16),
        in_specs=[vmem] * 3,
        out_specs=vmem,
        compiler_params=pltpu.CompilerParams(vmem_limit_bytes=8 << 20),
        cost_estimate=pl.CostEstimate(
            flops=4 * groups * rows * own.size, bytes_accessed=2 << 20, transcendentals=0
        ),
        name="project",
    )(gathered, own, pair)


def dispatch_kernel(
    parts_ref, residual_ref, ranks_ref, hidden_ref, sent_hbm, mask, staged, sems
):
    rows, features = residual_ref.shape
    span = parts_ref.shape[1] // AXES["z"]
    for z in range(AXES["z"]):
        for half in range(2):
            place = (2 * z + half) * span
            total = residual_ref[place : place + span, :].astype(jnp.float32)
            for s in range(4):
                part = parts_ref[2 * s + half, z * span : (z + 1) * span, :]
                total = total + part.astype(jnp.float32)
            hidden_ref[place : place + span, :] = total
    hidden = hidden_ref[...].astype(jnp.bfloat16)
    slot = lax.broadcasted_iota(jnp.int32, (CAP, rows), 0)
    step = GROUPS // sems.shape[0]
    copies = []
    for k in range(sems.shape[0]):
        for i in range(step):
            e = k * step + i
            mask[i * CAP : (i + 1) * CAP, :] = jnp.where(
                ranks_ref[e : e + 1, :] == slot, 1.0, 0.0
            ).astype(jnp.bfloat16)
        picked = jnp.dot(mask[...], hidden, preferred_element_type=jnp.float32)
        for i in range(step):
            staged[k * step + i] = picked[i * CAP : (i + 1) * CAP, :].astype(jnp.bfloat16)
        place = pl.ds(k * step, step)
        copies.append(pltpu.make_async_copy(staged.at[place], sent_hbm.at[place], sems.at[k]))
        copies[-1].start()
    for copy in copies:
        copy.wait()


def dispatch(parts, residual, ranks):
    vmem = pl.BlockSpec(memory_space=pltpu.VMEM)
    rows, features = residual.shape
    pieces = 4
    return pl.pallas_call(
        dispatch_kernel,
        out_shape=[
            jax.ShapeDtypeStruct((rows, features), jnp.float32),
            pltpu.HBM((GROUPS, CAP, features), jnp.bfloat16),
        ],
        in_specs=[vmem] * 3,
        out_specs=[vmem, pl.BlockSpec(memory_space=pl.ANY)],
        scratch_shapes=[
            pltpu.VMEM((GROUPS // pieces * CAP, rows), jnp.bfloat16),
            pltpu.VMEM((GROUPS, CAP, features), jnp.bfloat16),
            pltpu.SemaphoreType.DMA((pieces,)),
        ],
        compiler_params=pltpu.CompilerParams(vmem_limit_bytes=8 << 20),
        cost_estimate=pl.CostEstimate(
            flops=2 * GROUPS * CAP * rows * features, bytes_accessed=2 << 20, transcendentals=0
        ),
        name="dispatch",
    )(parts, residual, ranks)


def sum_over_sec(part):
    pair = part + lax.ppermute(part, "core", SWAP)
    pair = pair.astype(jnp.bfloat16)
    return pair.astype(jnp.float32) + lax.ppermute(pair, "y_hi", SWAP).astype(jnp.float32)


def slot_tables(routes):
    expert_ids = jnp.arange(2 * GROUPS, dtype=jnp.int32)
    chosen = jnp.any(routes[:, :, None] == expert_ids, axis=1)
    earlier = jnp.tri(routes.shape[0], k=-1, dtype=jnp.bfloat16)
    rank = jnp.dot(earlier, chosen.astype(jnp.bfloat16), preferred_element_type=jnp.float32)
    return jnp.where(chosen, rank.astype(jnp.int32), -1).T


def one_hot(ranks):
    slot_ids = jnp.arange(CAP, dtype=jnp.int32)[None, :, None]
    return (ranks[:, None, :] == slot_ids).astype(jnp.bfloat16)


def shards(
    queries,
    fresh_key_value,
    key_value_cache,
    lengths,
    residual,
    out_weight,
    norm_gain,
    routes,
    route_weights,
    w_gate,
    w_up,
    w_down,
):
    row_count = routes.shape[0]
    width = queries.shape[1]
    core = lax.axis_index("core")
    half = lax.axis_index("y_lo")
    group = lax.axis_index(DEV)
    blocks = attend(queries, fresh_key_value, key_value_cache, lengths, norm_gain)
    blocks, late_weight = lax.optimization_barrier((blocks, out_weight))
    pair_weight = lax.ppermute(late_weight, "y_lo", SWAP)
    gathered = exchange(blocks, ("z", "x"))
    parts = exchange(project(gathered, out_weight, pair_weight), ("y_hi", "core", "y_lo"))
    own_gain = jnp.sum(gathered[:, :3, width:].astype(jnp.float32), axis=1)
    pair_gain = lax.ppermute(own_gain, "y_lo", SWAP)
    ranks = slot_tables(routes).reshape(GROUPS, 2, row_count)
    own_ranks = lax.dynamic_index_in_dim(ranks, core, 1, keepdims=False)
    other_ranks = lax.dynamic_index_in_dim(ranks, 1 - core, 1, keepdims=False)
    hidden, sent = dispatch(parts, residual, own_ranks)
    sent, pair_gain, late_gate, late_up = lax.optimization_barrier(
        (sent, pair_gain, w_gate, w_up)
    )
    first_gate, first_up = preload(late_gate, late_up, FIRST)
    own_rows = exchange(sent, DEV)
    gain = jnp.where(half == 0, jnp.stack([own_gain, pair_gain]), jnp.stack([pair_gain, own_gain]))
    gain = gain.reshape(2, AXES["z"], AXES["x"], HEAD_SIZE).transpose(1, 0, 2, 3)
    gain = gain.reshape(GROUPS, HEAD_SIZE)
    other_rows = lax.ppermute(own_rows, "core", SWAP)

    local_ids = 2 * group + jnp.arange(2, dtype=jnp.int32)
    local_ranks = lax.dynamic_index_in_dim(ranks, group, 0, keepdims=False)
    shares = jnp.sum(
        jnp.where(routes[None] == local_ids[:, None, None], route_weights[None], 0.0), axis=2
    )
    slot_share = jnp.sum(
        jnp.where(
            local_ranks[:, None, :] == jnp.arange(CAP, dtype=jnp.int32)[None, :, None],
            shares[:, None, :],
            0.0,
        ),
        axis=2,
    )

    share = slot_share[:, :, None]
    units = w_gate.shape[2]
    picked_shape = (CAP, D)
    gate_shape = (GATE_CHUNKS, D // GATE_CHUNKS, units)
    own_shape = (2, (D - FIRST) // 2, units)
    down_shape = (DOWN_CHUNKS, units, D // DOWN_CHUNKS)
    own_result, next_down = expert_call(
        own_expert_kernel,
        "own_expert",
        [(pltpu.VMEM, (CAP, D)), (pltpu.VMEM, down_shape)],
        [picked_shape, own_shape, own_shape, down_shape],
        [own_rows, gain, share, first_gate, first_up],
        [w_gate, w_up, w_down],
    )
    moved = lax.ppermute(own_result, "core", SWAP)
    (activation,) = expert_call(
        other_gate_kernel,
        "other_gate",
        [(pltpu.VMEM, (CAP, units))],
        [picked_shape, gate_shape, gate_shape],
        [other_rows, gain],
        [w_gate, w_up],
    )
    out_shape = (GROUPS, CAP, D // GROUPS)
    (summed,) = expert_call(
        other_down_kernel,
        "other_down",
        [(pltpu.HBM, out_shape)],
        [out_shape],
        [activation, moved, share, next_down],
        [],
    )
    returned = exchange(summed, DEV)
    mixture_part = jnp.einsum(
        "ekr,ekf->rf", one_hot(other_ranks), returned, preferred_element_type=jnp.float32
    )
    mixture = sum_over_sec(mixture_part)
    return (hidden + mixture).astype(jnp.bfloat16)


def solution(mesh):
    named = jax.sharding.Mesh(
        np.reshape(mesh.devices, tuple(AXES.values())), tuple(AXES)
    )
    return jax.shard_map(
        shards,
        mesh=named,
        in_specs=(
            P(DEV, SEC),
            P(None, DEV, SEC),
            P(None, DEV, None, SEC),
            P(DEV),
            P(None, DEV),
            P(SEC, DEV),
            P(DEV),
            P(),
            P(),
            P(DEV, None, SEC),
            P(DEV, None, SEC),
            P(DEV, SEC, None),
        ),
        out_specs=P(None, DEV),
        check_vma=False,
    )
```

```python
import functools
import math

import jax
import jax.numpy as jnp
import numpy as np
from jax import lax
from jax.experimental import pallas as pl
from jax.experimental.pallas import tpu as pltpu
from jax.sharding import PartitionSpec as P

D = 4096
QUERY_HEADS = 64
KEY_VALUE_HEADS = 4
HEAD_SIZE = 128
CAP = 64
GROUPS = 32
PLANE = 16
GATE_CHUNKS = 4
FIRST = 1536
DOWN_CHUNKS = 4
ROW_GROUP = 4
AXES = {"y_hi": 2, "core": 2, "z": 4, "y_lo": 2, "x": 4}
SEC = ("y_hi", "core")
DEV = ("z", "y_lo", "x")
SWAP = [(0, 1), (1, 0)]


def attend_kernel(
    lengths_hbm,
    queries_hbm,
    fresh_hbm,
    gain_hbm,
    cache_ref,
    block_ref,
    lengths_ref,
    queries_ref,
    fresh_ref,
    gain_ref,
    keys,
    values,
    head_queries,
    head_scores,
    head_outputs,
    staged,
    small_sems,
    key_sems,
    value_sems,
    block_sems,
):
    rows = queries_ref.shape[0]
    heads = queries_ref.shape[1] // HEAD_SIZE
    slots = keys.shape[1]
    scale = 1.0 / math.sqrt(HEAD_SIZE)
    groups = rows // ROW_GROUP
    spans = [pl.ds(g * ROW_GROUP, ROW_GROUP) for g in range(groups)]
    key_copies = [
        pltpu.make_async_copy(cache_ref.at[0, span], keys.at[span], key_sems.at[g])
        for g, span in enumerate(spans)
    ]
    value_copies = [
        pltpu.make_async_copy(cache_ref.at[1, span], values.at[span], value_sems.at[g])
        for g, span in enumerate(spans)
    ]
    small_copies = [
        pltpu.make_async_copy(source, target, small_sems.at[i])
        for i, (source, target) in enumerate(
            (
                (queries_hbm, queries_ref),
                (gain_hbm, gain_ref),
                (fresh_hbm, fresh_ref),
                (lengths_hbm, lengths_ref),
            )
        )
    ]
    for copy in small_copies + [c for pair in zip(key_copies, value_copies) for c in pair]:
        copy.start()
    for copy in small_copies:
        copy.wait()
    gain = gain_ref[...]
    high = gain.astype(jnp.bfloat16).astype(jnp.float32)
    middle = (gain - high).astype(jnp.bfloat16).astype(jnp.float32)
    low = gain - high - middle
    place = lax.broadcasted_iota(jnp.int32, (rows, HEAD_SIZE), 0)
    terms = jnp.where(
        place == 0, high, jnp.where(place == 1, middle, jnp.where(place == 2, low, 0.0))
    )
    staged[:, heads * HEAD_SIZE :] = terms.astype(jnp.bfloat16)
    for h in range(heads):
        head_queries[pl.ds(h, rows, stride=heads), :] = queries_ref[
            :, h * HEAD_SIZE : (h + 1) * HEAD_SIZE
        ].astype(jnp.float32)
    slot = lax.broadcasted_iota(jnp.int32, (heads, slots), 1)
    pending = {}

    def score(r):
        return lax.dot_general(
            head_queries[r * heads : (r + 1) * heads, :].astype(jnp.bfloat16),
            keys[r],
            (((1,), (1,)), ((), ())),
            preferred_element_type=jnp.float32,
        )

    def weigh(r, scores):
        own_key = fresh_ref[0, r : r + 1, :].astype(jnp.float32)
        own_score = (
            jnp.sum(
                head_queries[r * heads : (r + 1) * heads, :] * own_key, axis=1, keepdims=True
            )
            * scale
        )
        scores = jnp.where(slot < lengths_ref[r], scores * scale, -jnp.inf)
        row_max = jnp.maximum(jnp.max(scores, axis=1, keepdims=True), own_score)
        weight = jnp.exp(scores - row_max)
        own_weight = jnp.exp(own_score - row_max)
        normalizer = jnp.sum(weight, axis=1, keepdims=True) + own_weight
        return weight.astype(jnp.bfloat16), own_weight, normalizer

    def blend(r, weight, own_weight, normalizer):
        own_value = fresh_ref[1, r : r + 1, :].astype(jnp.float32)
        weighted = jnp.dot(weight, values[r], preferred_element_type=jnp.float32)
        head_outputs[r * heads : (r + 1) * heads, :] = (
            weighted + own_weight * own_value
        ) / normalizer

    scored, weighed = {}, {}
    members = lambda g: range(g * ROW_GROUP, (g + 1) * ROW_GROUP)
    for g in range(groups + 2):
        if g < groups:
            key_copies[g].wait()
        if g >= 2:
            value_copies[g - 2].wait()
        if g < groups:
            for r in members(g):
                scored[r] = score(r)
        if 1 <= g <= groups:
            for r in members(g - 1):
                weighed[r] = weigh(r, scored.pop(r))
        if g >= 2:
            for r in members(g - 2):
                blend(r, *weighed.pop(r))
    for h in range(heads):
        staged[:, h * HEAD_SIZE : (h + 1) * HEAD_SIZE] = head_outputs[
            pl.ds(h, rows, stride=heads), :
        ].astype(jnp.bfloat16)
    block_copies = [
        pltpu.make_async_copy(staged, block_ref.at[i], block_sems.at[i])
        for i in range(block_ref.shape[0])
    ]
    for copy in block_copies:
        copy.start()
    for copy in block_copies:
        copy.wait()


def attend(queries, fresh_key_value, key_value_cache, lengths, norm_gain):
    rows, width = queries.shape
    slots = key_value_cache.shape[2]
    heads = width // HEAD_SIZE
    operands = (lengths, queries, fresh_key_value, norm_gain.reshape(1, HEAD_SIZE), key_value_cache)
    return pl.pallas_call(
        attend_kernel,
        out_shape=jax.ShapeDtypeStruct((PLANE, rows, width + HEAD_SIZE), jnp.bfloat16),
        in_specs=[pl.BlockSpec(memory_space=pl.ANY)] * len(operands),
        out_specs=pl.BlockSpec(memory_space=pl.ANY),
        scratch_shapes=[
            pltpu.SMEM((rows,), jnp.int32),
            pltpu.VMEM(queries.shape, jnp.bfloat16),
            pltpu.VMEM(fresh_key_value.shape, jnp.bfloat16),
            pltpu.VMEM((1, HEAD_SIZE), jnp.float32),
            pltpu.VMEM((rows, slots, HEAD_SIZE), jnp.bfloat16),
            pltpu.VMEM((rows, slots, HEAD_SIZE), jnp.bfloat16),
            pltpu.VMEM((rows * heads, HEAD_SIZE), jnp.float32),
            pltpu.VMEM((rows * heads, slots), jnp.float32),
            pltpu.VMEM((rows * heads, HEAD_SIZE), jnp.float32),
            pltpu.VMEM((rows, width + HEAD_SIZE), jnp.bfloat16),
            pltpu.SemaphoreType.DMA((4,)),
            pltpu.SemaphoreType.DMA((rows,)),
            pltpu.SemaphoreType.DMA((rows,)),
            pltpu.SemaphoreType.DMA((PLANE,)),
        ],
        compiler_params=pltpu.CompilerParams(vmem_limit_bytes=12 << 20),
        cost_estimate=pl.CostEstimate(
            flops=4 * rows * heads * slots * HEAD_SIZE,
            bytes_accessed=5 << 20,
            transcendentals=rows * heads * slots,
        ),
        name="attend",
    )(*(pltpu.with_memory_space_constraint(operand, pltpu.HBM) for operand in operands))


def land(copies):
    for copy in copies:
        copy.wait()
        yield


def in_order(copies, meanwhile):
    for copy in copies:
        copy.start()
    meanwhile()
    return land(copies)


def fill_picked(rows_ref, gain_ref, picked):
    groups, cap, width = rows_ref.shape
    square = jnp.zeros((cap, width), jnp.float32)
    for g in range(groups):
        part = rows_ref[g].astype(jnp.float32)
        square = square + part * part
    factor = lax.rsqrt(jnp.sum(square, axis=1, keepdims=True) / D + 1e-06)
    for g in range(groups):
        part = rows_ref[g].astype(jnp.float32)
        picked[:, g * width : (g + 1) * width] = (
            part * factor * gain_ref[g : g + 1, :]
        ).astype(jnp.bfloat16)


def row_copies(source, expert, target, sems, skipped=0):
    count, size = target.shape[0], target.shape[1]
    return [
        pltpu.make_async_copy(
            source.at[expert, pl.ds(skipped + k * size, size)], target.at[k], sems.at[k]
        )
        for k in range(count)
    ]


def column_copies(source, expert, target, sems):
    count, size = target.shape[0], target.shape[2]
    return [
        pltpu.make_async_copy(
            source.at[expert, :, pl.ds(k * size, size)], target.at[k], sems.at[k]
        )
        for k in range(count)
    ]


def activate(picked, gates, ups, landed, skipped):
    gate_sum = up_sum = None
    start = 0
    for k, (gate, up) in enumerate(zip(gates, ups)):
        part = picked[:, start : start + gate.shape[0]]
        start += gate.shape[0]
        if k >= skipped:
            next(landed)
        product = jnp.dot(part, gate[...], preferred_element_type=jnp.float32)
        gate_sum = product if gate_sum is None else gate_sum + product
        if k >= skipped:
            next(landed)
        product = jnp.dot(part, up[...], preferred_element_type=jnp.float32)
        up_sum = product if up_sum is None else up_sum + product
    return (gate_sum / (1.0 + jnp.exp(-gate_sum)) * up_sum).astype(jnp.bfloat16)


def parts_of(array):
    return [array.at[k] for k in range(array.shape[0])]


def paired(first, second):
    return [copy for pair in zip(first, second) for copy in pair]


def preload_kernel(gate_hbm, up_hbm, gate_ref, up_ref, sems):
    expert = lax.axis_index("core")
    place = pl.ds(0, gate_ref.shape[0])
    copies = [
        pltpu.make_async_copy(gate_hbm.at[expert, place], gate_ref, sems.at[0]),
        pltpu.make_async_copy(up_hbm.at[expert, place], up_ref, sems.at[1]),
    ]
    for copy in copies:
        copy.start()
    for copy in copies:
        copy.wait()


def preload(gate, up, rows):
    shape = (rows, gate.shape[2])
    return pl.pallas_call(
        preload_kernel,
        out_shape=[pltpu.VMEM(shape, jnp.bfloat16)] * 2,
        in_specs=[pl.BlockSpec(memory_space=pl.ANY)] * 2,
        out_specs=[pl.BlockSpec(memory_space=pltpu.VMEM)] * 2,
        scratch_shapes=[pltpu.SemaphoreType.DMA((2,))],
        compiler_params=pltpu.CompilerParams(vmem_limit_bytes=1 << 20),
        cost_estimate=pl.CostEstimate(
            flops=0, bytes_accessed=8 * rows * gate.shape[2], transcendentals=0
        ),
        name="preload",
    )(
        pltpu.with_memory_space_constraint(gate, pltpu.HBM),
        pltpu.with_memory_space_constraint(up, pltpu.HBM),
    )


def own_expert_kernel(
    rows_ref,
    gain_ref,
    share_ref,
    first_gate,
    first_up,
    gate_hbm,
    up_hbm,
    down_hbm,
    out_ref,
    next_down,
    picked,
    gate,
    up,
    down,
    sems,
):
    expert = lax.axis_index("core")
    skipped = first_gate.shape[0]
    gate_copies = row_copies(gate_hbm, expert, gate, sems.at[0], skipped)
    up_copies = row_copies(up_hbm, expert, up, sems.at[1], skipped)
    down_copies = column_copies(down_hbm, expert, down, sems.at[2])
    next_copies = column_copies(down_hbm, 1 - expert, next_down, sems.at[3])
    copies = paired(gate_copies, up_copies) + down_copies + next_copies
    landed = in_order(copies, functools.partial(fill_picked, rows_ref, gain_ref, picked))
    activation = activate(
        picked, [first_gate] + parts_of(gate), [first_up] + parts_of(up), landed, 1
    )
    share = share_ref[expert]
    step = down.shape[2]
    for k in range(down.shape[0]):
        next(landed)
        part = jnp.dot(activation, down[k], preferred_element_type=jnp.float32)
        out_ref[:, k * step : (k + 1) * step] = (part * share).astype(jnp.bfloat16)
    for _ in landed:
        pass


def other_gate_kernel(rows_ref, gain_ref, gate_hbm, up_hbm, out_ref, picked, gate, up, sems):
    expert = 1 - lax.axis_index("core")
    gate_copies = row_copies(gate_hbm, expert, gate, sems.at[0])
    up_copies = row_copies(up_hbm, expert, up, sems.at[1])
    landed = in_order(
        paired(gate_copies, up_copies), functools.partial(fill_picked, rows_ref, gain_ref, picked)
    )
    out_ref[...] = activate(picked, parts_of(gate), parts_of(up), landed, 0)
    for _ in landed:
        pass


def other_down_kernel(activation_ref, moved_ref, share_ref, down, out_hbm, staged, sems):
    expert = 1 - lax.axis_index("core")
    share = share_ref[expert]
    activation = activation_ref[...]
    width = staged.shape[2]
    step = down.shape[2]
    groups = step // width
    copies = []
    for k in range(down.shape[0]):
        part = jnp.dot(activation, down[k], preferred_element_type=jnp.float32)
        part = part * share + moved_ref[:, k * step : (k + 1) * step].astype(jnp.float32)
        for g in range(groups):
            staged[k * groups + g] = part[:, g * width : (g + 1) * width].astype(jnp.bfloat16)
        place = pl.ds(k * groups, groups)
        copies.append(pltpu.make_async_copy(staged.at[place], out_hbm.at[place], sems.at[0, k]))
        copies[-1].start()
    for copy in copies:
        copy.wait()


def expert_call(kernel, name, outs, scratch, small, weights):
    vmem = pl.BlockSpec(memory_space=pltpu.VMEM)
    any_space = pl.BlockSpec(memory_space=pl.ANY)
    size = sum(weight.size // 2 for weight in weights)
    return pl.pallas_call(
        kernel,
        out_shape=[space(shape, jnp.bfloat16) for space, shape in outs],
        in_specs=[vmem] * len(small) + [any_space] * len(weights),
        out_specs=[vmem if space is pltpu.VMEM else any_space for space, _ in outs],
        scratch_shapes=[pltpu.VMEM(shape, jnp.bfloat16) for shape in scratch]
        + [pltpu.SemaphoreType.DMA((4, max(GATE_CHUNKS, DOWN_CHUNKS)))],
        compiler_params=pltpu.CompilerParams(vmem_limit_bytes=16 << 20),
        cost_estimate=pl.CostEstimate(
            flops=2 * CAP * size, bytes_accessed=2 * size, transcendentals=0
        ),
        name=name,
    )(
        *(pltpu.with_memory_space_constraint(array, pltpu.VMEM) for array in small),
        *(pltpu.with_memory_space_constraint(array, pltpu.HBM) for array in weights),
    )


def exchange(blocks, axes):
    return lax.all_to_all(blocks, axes, 0, 0, tiled=True)


def project_kernel(gathered_ref, own_ref, pair_ref, out_ref):
    half = lax.axis_index("y_lo")
    rows, width = out_ref.shape[1], own_ref.shape[0]
    attn = gathered_ref[:, :, :width].reshape(rows, width)
    own = jnp.dot(attn, own_ref[...], preferred_element_type=jnp.float32).astype(jnp.bfloat16)
    pair = jnp.dot(attn, pair_ref[...], preferred_element_type=jnp.float32).astype(jnp.bfloat16)
    for s in range(out_ref.shape[0] // 2):
        out_ref[2 * s + half] = own
        out_ref[2 * s + 1 - half] = pair


def project(gathered, own, pair):
    vmem = pl.BlockSpec(memory_space=pltpu.VMEM)
    groups, rows, _ = gathered.shape
    width, features = own.shape
    return pl.pallas_call(
        project_kernel,
        out_shape=jax.ShapeDtypeStruct((8, groups * rows, features), jnp.bfloat16),
        in_specs=[vmem] * 3,
        out_specs=vmem,
        compiler_params=pltpu.CompilerParams(vmem_limit_bytes=8 << 20),
        cost_estimate=pl.CostEstimate(
            flops=4 * groups * rows * own.size, bytes_accessed=2 << 20, transcendentals=0
        ),
        name="project",
    )(gathered, own, pair)


def dispatch_kernel(
    parts_ref, residual_ref, ranks_ref, hidden_ref, sent_hbm, mask, staged, sems
):
    rows, features = residual_ref.shape
    span = parts_ref.shape[1] // AXES["z"]
    for z in range(AXES["z"]):
        for half in range(2):
            place = (2 * z + half) * span
            total = residual_ref[place : place + span, :].astype(jnp.float32)
            for s in range(4):
                part = parts_ref[2 * s + half, z * span : (z + 1) * span, :]
                total = total + part.astype(jnp.float32)
            hidden_ref[place : place + span, :] = total
    hidden = hidden_ref[...].astype(jnp.bfloat16)
    slot = lax.broadcasted_iota(jnp.int32, (CAP, rows), 0)
    step = GROUPS // sems.shape[0]
    copies = []
    for k in range(sems.shape[0]):
        for i in range(step):
            e = k * step + i
            mask[i * CAP : (i + 1) * CAP, :] = jnp.where(
                ranks_ref[e : e + 1, :] == slot, 1.0, 0.0
            ).astype(jnp.bfloat16)
        picked = jnp.dot(mask[...], hidden, preferred_element_type=jnp.float32)
        for i in range(step):
            staged[k * step + i] = picked[i * CAP : (i + 1) * CAP, :].astype(jnp.bfloat16)
        place = pl.ds(k * step, step)
        copies.append(pltpu.make_async_copy(staged.at[place], sent_hbm.at[place], sems.at[k]))
        copies[-1].start()
    for copy in copies:
        copy.wait()


def dispatch(parts, residual, ranks):
    vmem = pl.BlockSpec(memory_space=pltpu.VMEM)
    rows, features = residual.shape
    pieces = 4
    return pl.pallas_call(
        dispatch_kernel,
        out_shape=[
            jax.ShapeDtypeStruct((rows, features), jnp.float32),
            pltpu.HBM((GROUPS, CAP, features), jnp.bfloat16),
        ],
        in_specs=[vmem] * 3,
        out_specs=[vmem, pl.BlockSpec(memory_space=pl.ANY)],
        scratch_shapes=[
            pltpu.VMEM((GROUPS // pieces * CAP, rows), jnp.bfloat16),
            pltpu.VMEM((GROUPS, CAP, features), jnp.bfloat16),
            pltpu.SemaphoreType.DMA((pieces,)),
        ],
        compiler_params=pltpu.CompilerParams(vmem_limit_bytes=8 << 20),
        cost_estimate=pl.CostEstimate(
            flops=2 * GROUPS * CAP * rows * features, bytes_accessed=2 << 20, transcendentals=0
        ),
        name="dispatch",
    )(parts, residual, ranks)


def sum_over_sec(part):
    pair = part + lax.ppermute(part, "core", SWAP)
    pair = pair.astype(jnp.bfloat16)
    return pair.astype(jnp.float32) + lax.ppermute(pair, "y_hi", SWAP).astype(jnp.float32)


def slot_tables(routes):
    expert_ids = jnp.arange(2 * GROUPS, dtype=jnp.int32)
    chosen = jnp.any(routes[:, :, None] == expert_ids, axis=1)
    earlier = jnp.tri(routes.shape[0], k=-1, dtype=jnp.bfloat16)
    rank = jnp.dot(earlier, chosen.astype(jnp.bfloat16), preferred_element_type=jnp.float32)
    return jnp.where(chosen, rank.astype(jnp.int32), -1).T


def one_hot(ranks):
    slot_ids = jnp.arange(CAP, dtype=jnp.int32)[None, :, None]
    return (ranks[:, None, :] == slot_ids).astype(jnp.bfloat16)


def shards(
    queries,
    fresh_key_value,
    key_value_cache,
    lengths,
    residual,
    out_weight,
    norm_gain,
    routes,
    route_weights,
    w_gate,
    w_up,
    w_down,
):
    row_count = routes.shape[0]
    width = queries.shape[1]
    core = lax.axis_index("core")
    half = lax.axis_index("y_lo")
    group = lax.axis_index(DEV)
    blocks = attend(queries, fresh_key_value, key_value_cache, lengths, norm_gain)
    blocks, late_weight = lax.optimization_barrier((blocks, out_weight))
    pair_weight = lax.ppermute(late_weight, "y_lo", SWAP)
    gathered = exchange(blocks, ("z", "x"))
    parts = exchange(project(gathered, out_weight, pair_weight), ("y_hi", "core", "y_lo"))
    own_gain = jnp.sum(gathered[:, :3, width:].astype(jnp.float32), axis=1)
    pair_gain = lax.ppermute(own_gain, "y_lo", SWAP)
    ranks = slot_tables(routes).reshape(GROUPS, 2, row_count)
    own_ranks = lax.dynamic_index_in_dim(ranks, core, 1, keepdims=False)
    other_ranks = lax.dynamic_index_in_dim(ranks, 1 - core, 1, keepdims=False)
    hidden, sent = dispatch(parts, residual, own_ranks)
    sent, pair_gain, late_gate, late_up = lax.optimization_barrier(
        (sent, pair_gain, w_gate, w_up)
    )
    first_gate, first_up = preload(late_gate, late_up, FIRST)
    own_rows = exchange(sent, DEV)
    gain = jnp.where(half == 0, jnp.stack([own_gain, pair_gain]), jnp.stack([pair_gain, own_gain]))
    gain = gain.reshape(2, AXES["z"], AXES["x"], HEAD_SIZE).transpose(1, 0, 2, 3)
    gain = gain.reshape(GROUPS, HEAD_SIZE)
    other_rows = lax.ppermute(own_rows, "core", SWAP)

    local_ids = 2 * group + jnp.arange(2, dtype=jnp.int32)
    local_ranks = lax.dynamic_index_in_dim(ranks, group, 0, keepdims=False)
    shares = jnp.sum(
        jnp.where(routes[None] == local_ids[:, None, None], route_weights[None], 0.0), axis=2
    )
    slot_share = jnp.sum(
        jnp.where(
            local_ranks[:, None, :] == jnp.arange(CAP, dtype=jnp.int32)[None, :, None],
            shares[:, None, :],
            0.0,
        ),
        axis=2,
    )

    share = slot_share[:, :, None]
    units = w_gate.shape[2]
    picked_shape = (CAP, D)
    gate_shape = (GATE_CHUNKS, D // GATE_CHUNKS, units)
    own_shape = (2, (D - FIRST) // 2, units)
    down_shape = (DOWN_CHUNKS, units, D // DOWN_CHUNKS)
    own_result, next_down = expert_call(
        own_expert_kernel,
        "own_expert",
        [(pltpu.VMEM, (CAP, D)), (pltpu.VMEM, down_shape)],
        [picked_shape, own_shape, own_shape, down_shape],
        [own_rows, gain, share, first_gate, first_up],
        [w_gate, w_up, w_down],
    )
    moved = lax.ppermute(own_result, "core", SWAP)
    (activation,) = expert_call(
        other_gate_kernel,
        "other_gate",
        [(pltpu.VMEM, (CAP, units))],
        [picked_shape, gate_shape, gate_shape],
        [other_rows, gain],
        [w_gate, w_up],
    )
    out_shape = (GROUPS, CAP, D // GROUPS)
    (summed,) = expert_call(
        other_down_kernel,
        "other_down",
        [(pltpu.HBM, out_shape)],
        [out_shape],
        [activation, moved, share, next_down],
        [],
    )
    returned = exchange(summed, DEV)
    mixture_part = jnp.einsum(
        "ekr,ekf->rf", one_hot(other_ranks), returned, preferred_element_type=jnp.float32
    )
    mixture = sum_over_sec(mixture_part)
    return (hidden + mixture).astype(jnp.bfloat16)


def solution(mesh):
    named = jax.sharding.Mesh(
        np.reshape(mesh.devices, tuple(AXES.values())), tuple(AXES)
    )
    return jax.shard_map(
        shards,
        mesh=named,
        in_specs=(
            P(DEV, SEC),
            P(None, DEV, SEC),
            P(None, DEV, None, SEC),
            P(DEV),
            P(None, DEV),
            P(SEC, DEV),
            P(DEV),
            P(),
            P(),
            P(DEV, None, SEC),
            P(DEV, None, SEC),
            P(DEV, SEC, None),
        ),
        out_specs=P(None, DEV),
        check_vma=False,
    )
```

```python
import functools
import math

import jax
import jax.numpy as jnp
import numpy as np
from jax import lax
from jax.experimental import pallas as pl
from jax.experimental.pallas import tpu as pltpu
from jax.sharding import PartitionSpec as P

D = 4096
QUERY_HEADS = 64
KEY_VALUE_HEADS = 4
HEAD_SIZE = 128
CAP = 64
GROUPS = 32
PLANE = 16
GATE_CHUNKS = 4
FIRST = 1536
DOWN_CHUNKS = 2
ROW_GROUP = 4
AXES = {"y_hi": 2, "core": 2, "z": 4, "y_lo": 2, "x": 4}
SEC = ("y_hi", "core")
DEV = ("z", "y_lo", "x")
SWAP = [(0, 1), (1, 0)]


def attend_kernel(
    lengths_hbm,
    queries_hbm,
    fresh_hbm,
    gain_hbm,
    cache_ref,
    block_ref,
    lengths_ref,
    queries_ref,
    fresh_ref,
    gain_ref,
    keys,
    values,
    head_queries,
    head_scores,
    head_outputs,
    staged,
    small_sems,
    key_sems,
    value_sems,
    block_sems,
):
    rows = queries_ref.shape[0]
    heads = queries_ref.shape[1] // HEAD_SIZE
    slots = keys.shape[1]
    scale = 1.0 / math.sqrt(HEAD_SIZE)
    groups = rows // ROW_GROUP
    spans = [pl.ds(g * ROW_GROUP, ROW_GROUP) for g in range(groups)]
    key_copies = [
        pltpu.make_async_copy(cache_ref.at[0, span], keys.at[span], key_sems.at[g])
        for g, span in enumerate(spans)
    ]
    value_copies = [
        pltpu.make_async_copy(cache_ref.at[1, span], values.at[span], value_sems.at[g])
        for g, span in enumerate(spans)
    ]
    small_copies = [
        pltpu.make_async_copy(source, target, small_sems.at[i])
        for i, (source, target) in enumerate(
            (
                (queries_hbm, queries_ref),
                (gain_hbm, gain_ref),
                (fresh_hbm, fresh_ref),
                (lengths_hbm, lengths_ref),
            )
        )
    ]
    for copy in small_copies + [c for pair in zip(key_copies, value_copies) for c in pair]:
        copy.start()
    for copy in small_copies:
        copy.wait()
    gain = gain_ref[...]
    high = gain.astype(jnp.bfloat16).astype(jnp.float32)
    middle = (gain - high).astype(jnp.bfloat16).astype(jnp.float32)
    low = gain - high - middle
    place = lax.broadcasted_iota(jnp.int32, (rows, HEAD_SIZE), 0)
    terms = jnp.where(
        place == 0, high, jnp.where(place == 1, middle, jnp.where(place == 2, low, 0.0))
    )
    staged[:, heads * HEAD_SIZE :] = terms.astype(jnp.bfloat16)
    for h in range(heads):
        head_queries[pl.ds(h, rows, stride=heads), :] = queries_ref[
            :, h * HEAD_SIZE : (h + 1) * HEAD_SIZE
        ].astype(jnp.float32)
    slot = lax.broadcasted_iota(jnp.int32, (heads, slots), 1)
    pending = {}

    def score(r):
        return lax.dot_general(
            head_queries[r * heads : (r + 1) * heads, :].astype(jnp.bfloat16),
            keys[r],
            (((1,), (1,)), ((), ())),
            preferred_element_type=jnp.float32,
        )

    def weigh(r, scores):
        own_key = fresh_ref[0, r : r + 1, :].astype(jnp.float32)
        own_score = (
            jnp.sum(
                head_queries[r * heads : (r + 1) * heads, :] * own_key, axis=1, keepdims=True
            )
            * scale
        )
        scores = jnp.where(slot < lengths_ref[r], scores * scale, -jnp.inf)
        row_max = jnp.maximum(jnp.max(scores, axis=1, keepdims=True), own_score)
        weight = jnp.exp(scores - row_max)
        own_weight = jnp.exp(own_score - row_max)
        normalizer = jnp.sum(weight, axis=1, keepdims=True) + own_weight
        return weight.astype(jnp.bfloat16), own_weight, normalizer

    def blend(r, weight, own_weight, normalizer):
        own_value = fresh_ref[1, r : r + 1, :].astype(jnp.float32)
        weighted = jnp.dot(weight, values[r], preferred_element_type=jnp.float32)
        head_outputs[r * heads : (r + 1) * heads, :] = (
            weighted + own_weight * own_value
        ) / normalizer

    scored, weighed = {}, {}
    members = lambda g: range(g * ROW_GROUP, (g + 1) * ROW_GROUP)
    for g in range(groups + 2):
        if g < groups:
            key_copies[g].wait()
        if g >= 2:
            value_copies[g - 2].wait()
        if g < groups:
            for r in members(g):
                scored[r] = score(r)
        if 1 <= g <= groups:
            for r in members(g - 1):
                weighed[r] = weigh(r, scored.pop(r))
        if g >= 2:
            for r in members(g - 2):
                blend(r, *weighed.pop(r))
    for h in range(heads):
        staged[:, h * HEAD_SIZE : (h + 1) * HEAD_SIZE] = head_outputs[
            pl.ds(h, rows, stride=heads), :
        ].astype(jnp.bfloat16)
    block_copies = [
        pltpu.make_async_copy(staged, block_ref.at[i], block_sems.at[i])
        for i in range(block_ref.shape[0])
    ]
    for copy in block_copies:
        copy.start()
    for copy in block_copies:
        copy.wait()


def attend(queries, fresh_key_value, key_value_cache, lengths, norm_gain):
    rows, width = queries.shape
    slots = key_value_cache.shape[2]
    heads = width // HEAD_SIZE
    operands = (lengths, queries, fresh_key_value, norm_gain.reshape(1, HEAD_SIZE), key_value_cache)
    return pl.pallas_call(
        attend_kernel,
        out_shape=jax.ShapeDtypeStruct((PLANE, rows, width + HEAD_SIZE), jnp.bfloat16),
        in_specs=[pl.BlockSpec(memory_space=pl.ANY)] * len(operands),
        out_specs=pl.BlockSpec(memory_space=pl.ANY),
        scratch_shapes=[
            pltpu.SMEM((rows,), jnp.int32),
            pltpu.VMEM(queries.shape, jnp.bfloat16),
            pltpu.VMEM(fresh_key_value.shape, jnp.bfloat16),
            pltpu.VMEM((1, HEAD_SIZE), jnp.float32),
            pltpu.VMEM((rows, slots, HEAD_SIZE), jnp.bfloat16),
            pltpu.VMEM((rows, slots, HEAD_SIZE), jnp.bfloat16),
            pltpu.VMEM((rows * heads, HEAD_SIZE), jnp.float32),
            pltpu.VMEM((rows * heads, slots), jnp.float32),
            pltpu.VMEM((rows * heads, HEAD_SIZE), jnp.float32),
            pltpu.VMEM((rows, width + HEAD_SIZE), jnp.bfloat16),
            pltpu.SemaphoreType.DMA((4,)),
            pltpu.SemaphoreType.DMA((rows,)),
            pltpu.SemaphoreType.DMA((rows,)),
            pltpu.SemaphoreType.DMA((PLANE,)),
        ],
        compiler_params=pltpu.CompilerParams(vmem_limit_bytes=12 << 20),
        cost_estimate=pl.CostEstimate(
            flops=4 * rows * heads * slots * HEAD_SIZE,
            bytes_accessed=5 << 20,
            transcendentals=rows * heads * slots,
        ),
        name="attend",
    )(*(pltpu.with_memory_space_constraint(operand, pltpu.HBM) for operand in operands))


def land(copies):
    for copy in copies:
        copy.wait()
        yield


def in_order(copies, meanwhile):
    for copy in copies:
        copy.start()
    meanwhile()
    return land(copies)


def fill_picked(rows_ref, gain_ref, picked):
    groups, cap, width = rows_ref.shape
    square = jnp.zeros((cap, width), jnp.float32)
    for g in range(groups):
        part = rows_ref[g].astype(jnp.float32)
        square = square + part * part
    factor = lax.rsqrt(jnp.sum(square, axis=1, keepdims=True) / D + 1e-06)
    for g in range(groups):
        part = rows_ref[g].astype(jnp.float32)
        picked[:, g * width : (g + 1) * width] = (
            part * factor * gain_ref[g : g + 1, :]
        ).astype(jnp.bfloat16)


def row_copies(source, expert, target, sems, skipped=0):
    count, size = target.shape[0], target.shape[1]
    return [
        pltpu.make_async_copy(
            source.at[expert, pl.ds(skipped + k * size, size)], target.at[k], sems.at[k]
        )
        for k in range(count)
    ]


def column_copies(source, expert, target, sems):
    count, size = target.shape[0], target.shape[2]
    return [
        pltpu.make_async_copy(
            source.at[expert, :, pl.ds(k * size, size)], target.at[k], sems.at[k]
        )
        for k in range(count)
    ]


def activate(picked, gates, ups, landed, skipped):
    gate_sum = up_sum = None
    start = 0
    for k, (gate, up) in enumerate(zip(gates, ups)):
        part = picked[:, start : start + gate.shape[0]]
        start += gate.shape[0]
        if k >= skipped:
            next(landed)
        product = jnp.dot(part, gate[...], preferred_element_type=jnp.float32)
        gate_sum = product if gate_sum is None else gate_sum + product
        if k >= skipped:
            next(landed)
        product = jnp.dot(part, up[...], preferred_element_type=jnp.float32)
        up_sum = product if up_sum is None else up_sum + product
    return (gate_sum / (1.0 + jnp.exp(-gate_sum)) * up_sum).astype(jnp.bfloat16)


def parts_of(array):
    return [array.at[k] for k in range(array.shape[0])]


def paired(first, second):
    return [copy for pair in zip(first, second) for copy in pair]


def preload_kernel(gate_hbm, up_hbm, gate_ref, up_ref, sems):
    expert = lax.axis_index("core")
    place = pl.ds(0, gate_ref.shape[0])
    copies = [
        pltpu.make_async_copy(gate_hbm.at[expert, place], gate_ref, sems.at[0]),
        pltpu.make_async_copy(up_hbm.at[expert, place], up_ref, sems.at[1]),
    ]
    for copy in copies:
        copy.start()
    for copy in copies:
        copy.wait()


def preload(gate, up, rows):
    shape = (rows, gate.shape[2])
    return pl.pallas_call(
        preload_kernel,
        out_shape=[pltpu.VMEM(shape, jnp.bfloat16)] * 2,
        in_specs=[pl.BlockSpec(memory_space=pl.ANY)] * 2,
        out_specs=[pl.BlockSpec(memory_space=pltpu.VMEM)] * 2,
        scratch_shapes=[pltpu.SemaphoreType.DMA((2,))],
        compiler_params=pltpu.CompilerParams(vmem_limit_bytes=1 << 20),
        cost_estimate=pl.CostEstimate(
            flops=0, bytes_accessed=8 * rows * gate.shape[2], transcendentals=0
        ),
        name="preload",
    )(
        pltpu.with_memory_space_constraint(gate, pltpu.HBM),
        pltpu.with_memory_space_constraint(up, pltpu.HBM),
    )


def own_expert_kernel(
    rows_ref,
    gain_ref,
    share_ref,
    first_gate,
    first_up,
    gate_hbm,
    up_hbm,
    down_hbm,
    out_ref,
    next_down,
    picked,
    gate,
    up,
    down,
    sems,
):
    expert = lax.axis_index("core")
    skipped = first_gate.shape[0]
    gate_copies = row_copies(gate_hbm, expert, gate, sems.at[0], skipped)
    up_copies = row_copies(up_hbm, expert, up, sems.at[1], skipped)
    down_copies = column_copies(down_hbm, expert, down, sems.at[2])
    next_copies = column_copies(down_hbm, 1 - expert, next_down, sems.at[3])
    copies = paired(gate_copies, up_copies) + down_copies + next_copies
    landed = in_order(copies, functools.partial(fill_picked, rows_ref, gain_ref, picked))
    activation = activate(
        picked, [first_gate] + parts_of(gate), [first_up] + parts_of(up), landed, 1
    )
    share = share_ref[expert]
    step = down.shape[2]
    for k in range(down.shape[0]):
        next(landed)
        part = jnp.dot(activation, down[k], preferred_element_type=jnp.float32)
        out_ref[:, k * step : (k + 1) * step] = (part * share).astype(jnp.bfloat16)
    for _ in landed:
        pass


def other_gate_kernel(rows_ref, gain_ref, gate_hbm, up_hbm, out_ref, picked, gate, up, sems):
    expert = 1 - lax.axis_index("core")
    gate_copies = row_copies(gate_hbm, expert, gate, sems.at[0])
    up_copies = row_copies(up_hbm, expert, up, sems.at[1])
    landed = in_order(
        paired(gate_copies, up_copies), functools.partial(fill_picked, rows_ref, gain_ref, picked)
    )
    out_ref[...] = activate(picked, parts_of(gate), parts_of(up), landed, 0)
    for _ in landed:
        pass


def other_down_kernel(activation_ref, moved_ref, share_ref, down, out_hbm, staged, sems):
    expert = 1 - lax.axis_index("core")
    share = share_ref[expert]
    activation = activation_ref[...]
    width = staged.shape[2]
    step = down.shape[2]
    groups = step // width
    copies = []
    for k in range(down.shape[0]):
        part = jnp.dot(activation, down[k], preferred_element_type=jnp.float32)
        part = part * share + moved_ref[:, k * step : (k + 1) * step].astype(jnp.float32)
        for g in range(groups):
            staged[k * groups + g] = part[:, g * width : (g + 1) * width].astype(jnp.bfloat16)
        place = pl.ds(k * groups, groups)
        copies.append(pltpu.make_async_copy(staged.at[place], out_hbm.at[place], sems.at[0, k]))
        copies[-1].start()
    for copy in copies:
        copy.wait()


def expert_call(kernel, name, outs, scratch, small, weights):
    vmem = pl.BlockSpec(memory_space=pltpu.VMEM)
    any_space = pl.BlockSpec(memory_space=pl.ANY)
    size = sum(weight.size // 2 for weight in weights)
    return pl.pallas_call(
        kernel,
        out_shape=[space(shape, jnp.bfloat16) for space, shape in outs],
        in_specs=[vmem] * len(small) + [any_space] * len(weights),
        out_specs=[vmem if space is pltpu.VMEM else any_space for space, _ in outs],
        scratch_shapes=[pltpu.VMEM(shape, jnp.bfloat16) for shape in scratch]
        + [pltpu.SemaphoreType.DMA((4, max(GATE_CHUNKS, DOWN_CHUNKS)))],
        compiler_params=pltpu.CompilerParams(vmem_limit_bytes=16 << 20),
        cost_estimate=pl.CostEstimate(
            flops=2 * CAP * size, bytes_accessed=2 * size, transcendentals=0
        ),
        name=name,
    )(
        *(pltpu.with_memory_space_constraint(array, pltpu.VMEM) for array in small),
        *(pltpu.with_memory_space_constraint(array, pltpu.HBM) for array in weights),
    )


def exchange(blocks, axes):
    return lax.all_to_all(blocks, axes, 0, 0, tiled=True)


def project_kernel(gathered_ref, own_ref, pair_ref, out_ref):
    half = lax.axis_index("y_lo")
    rows, width = out_ref.shape[1], own_ref.shape[0]
    attn = gathered_ref[:, :, :width].reshape(rows, width)
    own = jnp.dot(attn, own_ref[...], preferred_element_type=jnp.float32).astype(jnp.bfloat16)
    pair = jnp.dot(attn, pair_ref[...], preferred_element_type=jnp.float32).astype(jnp.bfloat16)
    for s in range(out_ref.shape[0] // 2):
        out_ref[2 * s + half] = own
        out_ref[2 * s + 1 - half] = pair


def project(gathered, own, pair):
    vmem = pl.BlockSpec(memory_space=pltpu.VMEM)
    groups, rows, _ = gathered.shape
    width, features = own.shape
    return pl.pallas_call(
        project_kernel,
        out_shape=jax.ShapeDtypeStruct((8, groups * rows, features), jnp.bfloat16),
        in_specs=[vmem] * 3,
        out_specs=vmem,
        compiler_params=pltpu.CompilerParams(vmem_limit_bytes=8 << 20),
        cost_estimate=pl.CostEstimate(
            flops=4 * groups * rows * own.size, bytes_accessed=2 << 20, transcendentals=0
        ),
        name="project",
    )(gathered, own, pair)


def dispatch_kernel(
    parts_ref, residual_ref, ranks_ref, hidden_ref, sent_hbm, mask, staged, sems
):
    rows, features = residual_ref.shape
    span = parts_ref.shape[1] // AXES["z"]
    for z in range(AXES["z"]):
        for half in range(2):
            place = (2 * z + half) * span
            total = residual_ref[place : place + span, :].astype(jnp.float32)
            for s in range(4):
                part = parts_ref[2 * s + half, z * span : (z + 1) * span, :]
                total = total + part.astype(jnp.float32)
            hidden_ref[place : place + span, :] = total
    hidden = hidden_ref[...].astype(jnp.bfloat16)
    slot = lax.broadcasted_iota(jnp.int32, (CAP, rows), 0)
    step = GROUPS // sems.shape[0]
    copies = []
    for k in range(sems.shape[0]):
        for i in range(step):
            e = k * step + i
            mask[i * CAP : (i + 1) * CAP, :] = jnp.where(
                ranks_ref[e : e + 1, :] == slot, 1.0, 0.0
            ).astype(jnp.bfloat16)
        picked = jnp.dot(mask[...], hidden, preferred_element_type=jnp.float32)
        for i in range(step):
            staged[k * step + i] = picked[i * CAP : (i + 1) * CAP, :].astype(jnp.bfloat16)
        place = pl.ds(k * step, step)
        copies.append(pltpu.make_async_copy(staged.at[place], sent_hbm.at[place], sems.at[k]))
        copies[-1].start()
    for copy in copies:
        copy.wait()


def dispatch(parts, residual, ranks):
    vmem = pl.BlockSpec(memory_space=pltpu.VMEM)
    rows, features = residual.shape
    pieces = 4
    return pl.pallas_call(
        dispatch_kernel,
        out_shape=[
            jax.ShapeDtypeStruct((rows, features), jnp.float32),
            pltpu.HBM((GROUPS, CAP, features), jnp.bfloat16),
        ],
        in_specs=[vmem] * 3,
        out_specs=[vmem, pl.BlockSpec(memory_space=pl.ANY)],
        scratch_shapes=[
            pltpu.VMEM((GROUPS // pieces * CAP, rows), jnp.bfloat16),
            pltpu.VMEM((GROUPS, CAP, features), jnp.bfloat16),
            pltpu.SemaphoreType.DMA((pieces,)),
        ],
        compiler_params=pltpu.CompilerParams(vmem_limit_bytes=8 << 20),
        cost_estimate=pl.CostEstimate(
            flops=2 * GROUPS * CAP * rows * features, bytes_accessed=2 << 20, transcendentals=0
        ),
        name="dispatch",
    )(parts, residual, ranks)


def sum_over_sec(part):
    half = part.astype(jnp.bfloat16)
    pair = half.astype(jnp.float32) + lax.ppermute(half, "core", SWAP).astype(jnp.float32)
    pair = pair.astype(jnp.bfloat16)
    return pair.astype(jnp.float32) + lax.ppermute(pair, "y_hi", SWAP).astype(jnp.float32)


def slot_tables(routes):
    expert_ids = jnp.arange(2 * GROUPS, dtype=jnp.int32)
    chosen = jnp.any(routes[:, :, None] == expert_ids, axis=1)
    earlier = jnp.tri(routes.shape[0], k=-1, dtype=jnp.bfloat16)
    rank = jnp.dot(earlier, chosen.astype(jnp.bfloat16), preferred_element_type=jnp.float32)
    return jnp.where(chosen, rank.astype(jnp.int32), -1).T


def one_hot(ranks):
    slot_ids = jnp.arange(CAP, dtype=jnp.int32)[None, :, None]
    return (ranks[:, None, :] == slot_ids).astype(jnp.bfloat16)


def shards(
    queries,
    fresh_key_value,
    key_value_cache,
    lengths,
    residual,
    out_weight,
    norm_gain,
    routes,
    route_weights,
    w_gate,
    w_up,
    w_down,
):
    row_count = routes.shape[0]
    width = queries.shape[1]
    core = lax.axis_index("core")
    half = lax.axis_index("y_lo")
    group = lax.axis_index(DEV)
    blocks = attend(queries, fresh_key_value, key_value_cache, lengths, norm_gain)
    blocks, late_weight = lax.optimization_barrier((blocks, out_weight))
    pair_weight = lax.ppermute(late_weight, "y_lo", SWAP)
    gathered = exchange(blocks, ("z", "x"))
    parts = exchange(project(gathered, out_weight, pair_weight), ("y_hi", "core", "y_lo"))
    own_gain = jnp.sum(gathered[:, :3, width:].astype(jnp.float32), axis=1)
    pair_gain = lax.ppermute(own_gain, "y_lo", SWAP)
    ranks = slot_tables(routes).reshape(GROUPS, 2, row_count)
    own_ranks = lax.dynamic_index_in_dim(ranks, core, 1, keepdims=False)
    other_ranks = lax.dynamic_index_in_dim(ranks, 1 - core, 1, keepdims=False)
    hidden, sent = dispatch(parts, residual, own_ranks)
    sent, pair_gain, late_gate, late_up = lax.optimization_barrier(
        (sent, pair_gain, w_gate, w_up)
    )
    first_gate, first_up = preload(late_gate, late_up, FIRST)
    own_rows = exchange(sent, DEV)
    gain = jnp.where(half == 0, jnp.stack([own_gain, pair_gain]), jnp.stack([pair_gain, own_gain]))
    gain = gain.reshape(2, AXES["z"], AXES["x"], HEAD_SIZE).transpose(1, 0, 2, 3)
    gain = gain.reshape(GROUPS, HEAD_SIZE)
    other_rows = lax.ppermute(own_rows, "core", SWAP)

    local_ids = 2 * group + jnp.arange(2, dtype=jnp.int32)
    local_ranks = lax.dynamic_index_in_dim(ranks, group, 0, keepdims=False)
    shares = jnp.sum(
        jnp.where(routes[None] == local_ids[:, None, None], route_weights[None], 0.0), axis=2
    )
    slot_share = jnp.sum(
        jnp.where(
            local_ranks[:, None, :] == jnp.arange(CAP, dtype=jnp.int32)[None, :, None],
            shares[:, None, :],
            0.0,
        ),
        axis=2,
    )

    share = slot_share[:, :, None]
    units = w_gate.shape[2]
    picked_shape = (CAP, D)
    gate_shape = (GATE_CHUNKS, D // GATE_CHUNKS, units)
    own_shape = (2, (D - FIRST) // 2, units)
    down_shape = (DOWN_CHUNKS, units, D // DOWN_CHUNKS)
    own_result, next_down = expert_call(
        own_expert_kernel,
        "own_expert",
        [(pltpu.VMEM, (CAP, D)), (pltpu.VMEM, down_shape)],
        [picked_shape, own_shape, own_shape, down_shape],
        [own_rows, gain, share, first_gate, first_up],
        [w_gate, w_up, w_down],
    )
    moved = lax.ppermute(own_result, "core", SWAP)
    (activation,) = expert_call(
        other_gate_kernel,
        "other_gate",
        [(pltpu.VMEM, (CAP, units))],
        [picked_shape, gate_shape, gate_shape],
        [other_rows, gain],
        [w_gate, w_up],
    )
    out_shape = (GROUPS, CAP, D // GROUPS)
    (summed,) = expert_call(
        other_down_kernel,
        "other_down",
        [(pltpu.HBM, out_shape)],
        [out_shape],
        [activation, moved, share, next_down],
        [],
    )
    returned = exchange(summed, DEV)
    mixture_part = jnp.einsum(
        "ekr,ekf->rf", one_hot(other_ranks), returned, preferred_element_type=jnp.float32
    )
    mixture = sum_over_sec(mixture_part)
    return (hidden + mixture).astype(jnp.bfloat16)


def solution(mesh):
    named = jax.sharding.Mesh(
        np.reshape(mesh.devices, tuple(AXES.values())), tuple(AXES)
    )
    return jax.shard_map(
        shards,
        mesh=named,
        in_specs=(
            P(DEV, SEC),
            P(None, DEV, SEC),
            P(None, DEV, None, SEC),
            P(DEV),
            P(None, DEV),
            P(SEC, DEV),
            P(DEV),
            P(),
            P(),
            P(DEV, None, SEC),
            P(DEV, None, SEC),
            P(DEV, SEC, None),
        ),
        out_specs=P(None, DEV),
        check_vma=False,
    )
```
